32 devices in a mesh: fsdp: 4 (over z), context: 4 (over y, x), tensor: 2 (over core).
Axes of the slice: x: 2, y: 2, z: 4, core: 2. Of those that a mesh axis runs over, the one named last changes fastest.
Arguments:
- hidden: bfloat16 [16384, 1024], P(('fsdp', 'context')), may hold values from -6 to 6
- d_mixed: bfloat16 [16384, 1024], P(('fsdp', 'context')), may hold values from -6 to 6
- seq_lengths: int32 [4, 3], P('fsdp'), may hold values from 1 to 2048, 4096 in all within a row
- norm_gain: float32 [1024], replicated, may hold values from 0.5 to 1.5
- w_gate: bfloat16 [1024, 2048], P(('fsdp', 'context'), 'tensor'), may hold values from -0.1875 to 0.1875
- w_x: bfloat16 [1024, 2048], P(('fsdp', 'context'), 'tensor'), may hold values from -0.1875 to 0.1875
- w_bc: bfloat16 [1024, 256], P(('fsdp', 'context')), may hold values from -0.1875 to 0.1875
- w_dt: bfloat16 [1024, 32], P(('fsdp', 'context'), 'tensor'), may hold values from -0.09375 to 0.09375
- conv_x: float32 [4, 2048], P(None, 'tensor'), may hold values from -2 to 2
- conv_x_bias: float32 [2048], P('tensor'), may hold values from -1.5 to 1.5
- conv_bc: float32 [4, 256], replicated, may hold values from -2 to 2
- conv_bc_bias: float32 [256], replicated, may hold values from -1.5 to 1.5
- dt_bias: float32 [32], P('tensor'), may hold values from -8 to -2.5
- a_log: float32 [32], P('tensor'), may hold values from 0 to 2.77
- d_skip: float32 [32], P('tensor'), may hold values from 0.5 to 1.5
- gate_gain: float32 [2048], P('tensor'), may hold values from 0.5 to 1.5
- w_out: bfloat16 [2048, 1024], P('tensor', ('fsdp', 'context')), may hold values from -0.125 to 0.125
Outputs:
- mixed: bfloat16 [16384, 1024], P(('fsdp', 'context'), 'tensor')
- grad_hidden: float32 [16384, 1024], P(('fsdp', 'context'), 'tensor')
- grad_norm_gain: float32 [1024], P('tensor')
- grad_w_gate: float32 [1024, 2048], P(('fsdp', 'context'), 'tensor')
- grad_w_x: float32 [1024, 2048], P(('fsdp', 'context'), 'tensor')
- grad_w_bc: float32 [1024, 256], P(('fsdp', 'context'))
- grad_w_dt: float32 [1024, 32], P(('fsdp', 'context'), 'tensor')
- grad_conv_x: float32 [4, 2048], P(None, 'tensor')
- grad_conv_x_bias: float32 [2048], P('tensor')
- grad_conv_bc: float32 [4, 256], replicated
- grad_conv_bc_bias: float32 [256], replicated
- grad_dt_bias: float32 [32], P('tensor')
- grad_a_log: float32 [32], P('tensor')
- grad_d_skip: float32 [32], P('tensor')
- grad_gate_gain: float32 [2048], P('tensor')
- grad_w_out: float32 [2048, 1024], P('tensor', ('fsdp', 'context'))
The draws below stay inside these ranges and needn't reach their ends.
Inputs may be any that keep to these rules, and one draw needn't show every extreme that they name: `seq_lengths`: row f lists, in order, the lengths of the 3 sequences packed into token group f; they add up to 4096, and the longest is exactly 2048.
All inputs are finite; a program needn't handle non-finite values.
Results may differ from the reference program's by a relative error of at most 0.02.
Values may be sent and summed in bfloat16 or wider, within the bound.
A program may use at most 320 MiB of HBM per device.

```python
import math
import jax
import jax.numpy as jnp
import numpy as np
from jax import lax

D = 1024
HEADS = 32
HEADDIM = 64
STATE = 128
INNER = 2048
CONV = 4
SPAN = 256
SEQS = 3
GROUP_TOK = 4096
MAX_LEN = 2048
TOKENS = 16384
N_FSDP = 4
N_TENSOR = 2


def draw_dt_bias(key, part):
    values = jax.random.uniform(key, (HEADS,), jnp.float32, -7.0, -2.5)
    return values


def levels(stream_key, shape, split, low, top_value):
    gain = 1.0
    for position, blocks in split:
        draws = jax.random.uniform(jax.random.fold_in(jax.random.fold_in(stream_key, 6), position), (blocks,), jnp.float32, low / len(split), top_value / len(split))
        gain = gain * jnp.repeat(jnp.exp(draws), shape[position] // blocks).reshape((-1,) + (1,) * (len(shape) - 1 - position))
    return gain


def split_up(count, total, reach, lean):
    loads = [(1 << 20) // math.isqrt(standing ** lean) + 1 for standing in range(2, count + 1)]
    rest, given = total - reach - (count - 1), [1] * (count - 1)
    while rest > 0:
        free = [i for i in range(count - 1) if given[i] < reach]
        pool, budget = sum([loads[i] for i in free]), rest
        for i in free:
            addition = min(reach - given[i], max(1, budget * loads[i] // pool), rest)
            given[i] = given[i] + addition
            rest = rest - addition
    return np.array([reach] + given)


def uneven(stream_key, count, total, most, lean):
    if count == 2:
        one = jax.random.randint(stream_key, (), max(1, total - most), min(most, total - 1) + 1)
        return jnp.stack([one, total - one])
    sizes = jnp.asarray(split_up(count, total, most, lean), jnp.int32)
    twos = (count - 1) // 2
    donor, sink = sizes[1:1 + 2 * twos:2], sizes[2:2 + 2 * twos:2]
    margin = jnp.minimum(donor - 1, most - sink)
    shifted = jax.random.randint(jax.random.fold_in(stream_key, 1), (twos,), 0, 1 << 20) % (margin + 1)
    sizes = sizes.at[1:1 + 2 * twos:2].set(donor - shifted).at[2:2 + 2 * twos:2].set(sink + shifted)
    return sizes[jax.random.permutation(jax.random.fold_in(stream_key, 2), count)]


def centred(own_key, dims, deviation, most, pieces=(), held_as=jnp.bfloat16):
    array = jax.random.normal(own_key, dims, jnp.float32) * deviation
    if len(pieces) > 0:
        array = levels(own_key, dims, pieces, -0.22, 0.18) * array
    return jnp.clip(array, min=-most, max=most).astype(held_as)


def setup_inputs(seed: int = 0) -> dict:
    splits = jax.random.split(jax.random.key(seed), 18)
    hidden = centred(splits[0], (TOKENS, D), 1.0, 6.0, ((0, 16),))
    d_mixed = centred(splits[1], (TOKENS, D), 1.0, 6.0, ((0, 16),))
    seq_lengths = jax.vmap(lambda own: uneven(own, SEQS, GROUP_TOK, MAX_LEN, 2))(jax.random.split(splits[2], N_FSDP)).reshape((N_FSDP, SEQS)).astype(jnp.int32)
    norm_gain = jnp.clip(1.0 + 0.1 * jax.random.normal(splits[3], (D,), jnp.float32), 0.5, 1.5)
    w_gate = centred(splits[4], (D, INNER), D ** -0.5, 0.1875, ((0, 16), (1, 2)))
    w_x = centred(splits[5], (D, INNER), D ** -0.5, 0.1875, ((0, 16), (1, 2)))
    w_bc = centred(splits[6], (D, 2 * STATE), D ** -0.5, 0.1875, ((0, 16),))
    w_dt = centred(splits[7], (D, HEADS), (4 * D) ** -0.5, 0.09375, ((0, 16), (1, 2)))
    conv_x = centred(splits[8], (CONV, INNER), 0.4, 2.0, ((1, 2),), jnp.float32)
    conv_x_bias = centred(splits[9], (INNER,), 0.3, 1.5, ((0, 2),), jnp.float32)
    conv_bc = centred(splits[10], (CONV, 2 * STATE), 0.4, 2.0, (), jnp.float32)
    conv_bc_bias = centred(splits[11], (2 * STATE,), 0.3, 1.5, (), jnp.float32)
    dt_bias = draw_dt_bias(jax.random.fold_in(splits[17], 71), 0)
    a_log = jnp.clip(2.77 * jax.random.uniform(splits[13], (HEADS,), jnp.float32) ** levels(splits[13], (HEADS,), ((0, 2),), -0.2, 0.2), 0.0, 2.77)
    d_skip = jnp.clip(0.5 + 1.0 * jax.random.uniform(splits[14], (HEADS,), jnp.float32) ** levels(splits[14], (HEADS,), ((0, 2),), -0.2, 0.2), 0.5, 1.5)
    gate_gain = jnp.clip(1.0 + 0.1 * jax.random.normal(splits[15], (INNER,), jnp.float32), 0.5, 1.5)
    w_out = centred(splits[16], (INNER, D), INNER ** -0.5, 0.125, ((0, 2), (1, 16)))
    return dict(hidden=hidden, d_mixed=d_mixed, seq_lengths=seq_lengths, norm_gain=norm_gain, w_gate=w_gate, w_x=w_x, w_bc=w_bc, w_dt=w_dt, conv_x=conv_x, conv_x_bias=conv_x_bias, conv_bc=conv_bc, conv_bc_bias=conv_bc_bias, dt_bias=dt_bias, a_log=a_log, d_skip=d_skip, gate_gain=gate_gain, w_out=w_out)


EPSILON = 1e-05
PRECISE = lax.Precision.HIGHEST

def segment_ids(lengths, positions):
    starts = jnp.cumsum(lengths).astype(jnp.int32) - lengths
    inside = (positions[:, None] >= starts[None, 1:]).astype(jnp.int32)
    counted = lax.optimization_barrier(jnp.sum(inside, axis=1)).astype(jnp.int32)
    return jnp.where(positions < 0, -1, counted).astype(jnp.int32)

def causal_conv(values, edge_values, weight, conv_shift, segment, edge_segment):
    tap_count = weight.shape[0]
    length = values.shape[0]
    joined = jnp.concatenate([edge_values, values], axis=0)
    joined_segment = jnp.concatenate([edge_segment, segment], axis=0)
    summed = jnp.zeros_like(values) + conv_shift[None, :]
    for offset in range(tap_count):
        matched = joined_segment[offset:offset + length] == segment
        summed = summed + jnp.where(matched[:, None], joined[offset:offset + length], 0.0) * weight[offset][None, :]
    return jax.nn.silu(summed)

def span_scan(x_heads, delta, decay_rate, b_rows, c_rows, segment, seg_before, state):
    length, head_count, head_size = x_heads.shape
    blocks = length // SPAN
    span_last = segment[SPAN - 1::SPAN]
    prev_segment = jnp.concatenate([seg_before[None], span_last[:-1]])
    stacked = (x_heads.reshape(blocks, SPAN, head_count, head_size), delta.reshape(blocks, SPAN, head_count), b_rows.reshape(blocks, SPAN, -1), c_rows.reshape(blocks, SPAN, -1), segment.reshape(blocks, SPAN), prev_segment)

    def advance(carried, block):
        x_block, dt_block, b_block, c_block, seg_block, seg_prev = block
        rates = (dt_block * decay_rate[None, :]).T
        cumulative = jnp.cumsum(rates, axis=1)
        indices = jnp.arange(SPAN)
        causal = (indices[:, None] >= indices[None, :]) & (seg_block[:, None] == seg_block[None, :])
        spread = jnp.where(causal[None], cumulative[:, :, None] - cumulative[:, None, :], 0.0)
        decay = jnp.where(causal[None], jnp.exp(spread), 0.0)
        scores = jnp.dot(c_block, b_block.T, precision=PRECISE)
        mixing = decay * scores[None] * dt_block.T[:, None, :]
        within = jnp.einsum('hts,shp->thp', mixing, x_block, precision=PRECISE)
        leading = jnp.where((seg_block == seg_prev)[None, :], jnp.exp(cumulative), 0.0)
        from_state = jnp.einsum('tn,hpn->thp', c_block, carried, precision=PRECISE) * leading.T[:, :, None]
        trailing = jnp.where((seg_block == seg_block[-1])[None, :], jnp.exp(cumulative[:, -1:] - cumulative), 0.0) * dt_block.T
        weighted = x_block * trailing.T[:, :, None]
        added = jnp.einsum('shp,sn->hpn', weighted, b_block, precision=PRECISE)
        renewed = leading[:, -1][:, None, None] * carried + added
        return (renewed, within + from_state)
    final_state, outputs = lax.scan(advance, state, stacked)
    return (outputs.reshape(length, head_count, head_size), final_state)

def mixer_core(x_act, bc_act, dt_input, z_input, dt_bias, a_log, d_skip, state, segment, seg_before):
    length = x_act.shape[0]
    head_count = dt_input.shape[1]
    x_heads = x_act.reshape(length, head_count, -1)
    delta = jax.nn.softplus(dt_input + dt_bias[None, :])
    decay_rate = -jnp.exp(a_log)
    state_width = bc_act.shape[1] // 2
    output, unused = span_scan(x_heads, delta, decay_rate, bc_act[:, :state_width], bc_act[:, state_width:], segment, seg_before, state)
    output = output + d_skip[None, :, None] * x_heads
    return output.reshape(length, -1) * jax.nn.silu(z_input)

def reference(hidden, d_mixed, seq_lengths, norm_gain, w_gate, w_x, w_bc, w_dt, conv_x, conv_x_bias, conv_bc, conv_bc_bias, dt_bias, a_log, d_skip, gate_gain, w_out):
    model_width = w_gate.shape[0]
    inner_width = w_gate.shape[1]
    head_count = w_dt.shape[1]
    group_tokens = GROUP_TOK
    hidden_groups = hidden.reshape(N_FSDP, group_tokens, model_width)
    dmix_groups = d_mixed.reshape(N_FSDP, group_tokens, model_width)
    conv_weight = jnp.concatenate([conv_x, conv_bc], axis=1)
    conv_shift = jnp.concatenate([conv_x_bias, conv_bc_bias])
    edge_values = jnp.zeros((CONV - 1, conv_weight.shape[1]), jnp.float32)
    positions = jnp.arange(group_tokens, dtype=jnp.int32)
    edge_positions = jnp.arange(CONV - 1, dtype=jnp.int32) - (CONV - 1)
    zero_state = jnp.zeros((head_count, HEADDIM, STATE), jnp.float32)
    seg_start = jnp.full((), -1, jnp.int32)

    def group_pass(sums, inputs):
        hidden_rows, dmix_rows, lengths = inputs
        segment = segment_ids(lengths, positions)
        edge_segment = segment_ids(lengths, edge_positions)
        widened = hidden_rows.astype(jnp.float32)
        row_scale = lax.rsqrt(lax.optimization_barrier(jnp.mean(widened * widened, axis=1, keepdims=True)) + EPSILON)
        normed = (widened * row_scale * norm_gain[None, :]).astype(jnp.bfloat16)
        z_proj = lax.optimization_barrier(jnp.dot(normed, w_gate, preferred_element_type=jnp.float32).astype(jnp.bfloat16))
        x_proj = jnp.dot(normed, w_x, preferred_element_type=jnp.float32).astype(jnp.bfloat16)
        bc_proj = jnp.dot(normed, w_bc, preferred_element_type=jnp.float32).astype(jnp.bfloat16)
        dt_proj = lax.optimization_barrier(jnp.dot(normed, w_dt, preferred_element_type=jnp.float32).astype(jnp.bfloat16))
        conv_input = lax.optimization_barrier(jnp.concatenate([x_proj, bc_proj], axis=1))

        def conv_piece(values, weight, shift_row):
            return causal_conv(values, edge_values, weight, shift_row, segment, edge_segment)
        activated, conv_back = jax.vjp(conv_piece, conv_input.astype(jnp.float32), conv_weight, conv_shift)
        act_rounded = lax.optimization_barrier(activated.astype(jnp.bfloat16))
        x_act = act_rounded[:, :inner_width].astype(jnp.float32)
        bc_act = act_rounded[:, inner_width:].astype(jnp.float32)
        z_input = z_proj.astype(jnp.float32)
        dt_input = dt_proj.astype(jnp.float32)

        def core(x_in, bc_in, dt_in, z_in, bias_in, alog_in, skip_in):
            return mixer_core(x_in, bc_in, dt_in, z_in, bias_in, alog_in, skip_in, zero_state, segment, seg_start)
        gated, core_back = jax.vjp(core, x_act, bc_act, dt_input, z_input, dt_bias, a_log, d_skip)
        gate_scale = lax.rsqrt(lax.optimization_barrier(jnp.mean(gated * gated, axis=1, keepdims=True)) + EPSILON)
        normed_out = (gated * gate_scale * gate_gain[None, :]).astype(jnp.bfloat16)
        partials = jnp.einsum('tgc,gcd->gtd', normed_out.reshape(group_tokens, N_TENSOR, -1).astype(jnp.float32), w_out.reshape(N_TENSOR, -1, model_width).astype(jnp.float32))
        partials = lax.optimization_barrier(partials.astype(jnp.bfloat16))
        mixed_rows = (widened + lax.optimization_barrier(jnp.sum(partials.astype(jnp.float32), axis=0))).astype(jnp.bfloat16)
        grad_norm_out = jnp.dot(dmix_rows, w_out.T, preferred_element_type=jnp.float32)
        out_term = jnp.dot(normed_out.T, dmix_rows, preferred_element_type=jnp.float32)
        gain_term = lax.optimization_barrier(jnp.sum(grad_norm_out * gated * gate_scale, axis=0))
        scaled_grad = grad_norm_out * gate_gain[None, :]
        grad_gated = gate_scale * scaled_grad - gated * gate_scale ** 3 * lax.optimization_barrier(jnp.mean(scaled_grad * gated, axis=1, keepdims=True))
        grad_xact, grad_bcact, grad_dtin, grad_zin, grad_dtbias, grad_alog, grad_dskip = core_back(grad_gated)
        grad_conv_in, grad_convw, grad_convb = conv_back(jnp.concatenate([grad_xact, grad_bcact], axis=1))
        grad_zb = grad_zin.astype(jnp.bfloat16)
        grad_xb = grad_conv_in[:, :inner_width].astype(jnp.bfloat16)
        grad_bcb = grad_conv_in[:, inner_width:].astype(jnp.bfloat16)
        grad_dtb = grad_dtin.astype(jnp.bfloat16)
        gate_term = jnp.dot(normed.T, grad_zb, preferred_element_type=jnp.float32)
        xin_term = jnp.dot(normed.T, grad_xb, preferred_element_type=jnp.float32)
        bc_term = jnp.dot(normed.T, grad_bcb, preferred_element_type=jnp.float32)
        dt_term = jnp.dot(normed.T, grad_dtb, preferred_element_type=jnp.float32)

        def block_terms(grad_rows, weight):
            return jnp.einsum('tgc,dgc->gtd', grad_rows.reshape(group_tokens, N_TENSOR, -1).astype(jnp.float32), weight.reshape(model_width, N_TENSOR, -1).astype(jnp.float32))
        head_parts = block_terms(grad_zb, w_gate) + block_terms(grad_xb, w_x) + block_terms(grad_dtb, w_dt)
        head_parts = head_parts + block_terms(grad_bcb, w_bc)
        head_parts = lax.optimization_barrier(head_parts.astype(jnp.bfloat16))
        grad_normed = lax.optimization_barrier(jnp.sum(head_parts.astype(jnp.float32), axis=0))
        norm_term = lax.optimization_barrier(jnp.sum(grad_normed * widened * row_scale, axis=0))
        gained = grad_normed * norm_gain[None, :]
        grad_rows = dmix_rows.astype(jnp.float32) + row_scale * gained - widened * row_scale ** 3 * lax.optimization_barrier(jnp.mean(gained * widened, axis=1, keepdims=True))
        terms = (norm_term, gate_term, xin_term, bc_term, dt_term, grad_convw[:, :inner_width], grad_convb[:inner_width], grad_convw[:, inner_width:], grad_convb[inner_width:], grad_dtbias, grad_alog, grad_dskip, gain_term, out_term)
        renewed = tuple((older + newer for older, newer in zip(sums, terms)))
        return (renewed, (mixed_rows, grad_rows))
    start_sums = (jnp.zeros_like(norm_gain), jnp.zeros(w_gate.shape, jnp.float32), jnp.zeros(w_x.shape, jnp.float32), jnp.zeros(w_bc.shape, jnp.float32), jnp.zeros(w_dt.shape, jnp.float32), jnp.zeros_like(conv_x), jnp.zeros_like(conv_x_bias), jnp.zeros_like(conv_bc), jnp.zeros_like(conv_bc_bias), jnp.zeros_like(dt_bias), jnp.zeros_like(a_log), jnp.zeros_like(d_skip), jnp.zeros_like(gate_gain), jnp.zeros(w_out.shape, jnp.float32))
    sums, outputs = lax.scan(group_pass, start_sums, (hidden_groups, dmix_groups, seq_lengths))
    mixed = outputs[0].reshape(-1, model_width)
    grad_hidden = outputs[1].reshape(-1, model_width)
    return (mixed, grad_hidden, sums[0], sums[1], sums[2], sums[3], sums[4], sums[5], sums[6], sums[7], sums[8], sums[9], sums[10], sums[11], sums[12], sums[13])
```

```python
import functools
import jax
import jax.numpy as jnp
from jax import lax
from jax.experimental import pallas as pl
from jax.experimental.pallas import tpu as pltpu
from jax.sharding import PartitionSpec as P

EPSILON = 1e-05
HIGH = lax.Precision.HIGHEST
BF = jnp.bfloat16
F32 = jnp.float32
CHUNK = 128
NEG = -1e30
MESH = pl.DeviceIdType.MESH
NT = (((1,), (1,)), ((), ()))
TN = (((0,), (0,)), ((), ()))


def dot(a, b, dims=(((1,), (0,)), ((), ())), precision=None):
    return lax.dot_general(a, b, dims, precision=precision, preferred_element_type=F32)


def split2(value):
    high = value.astype(BF)
    return high, (value - high.astype(F32)).astype(BF)


def expand(value, spread):
    high, low = split2(value)
    return dot(high, spread) + dot(low, spread)


def per_head(value, spread):
    high, low = split2(value)
    return dot(high, spread, NT) + dot(low, spread, NT)


def seg_at(info_ref, count, positions):
    found = jnp.where(positions < 0, -1, 0)
    for k in range(1, count):
        found = found + jnp.where(positions >= info_ref[k], 1, 0)
    return found


def softplus(v):
    return jnp.maximum(v, 0.0) + jnp.log1p(jnp.exp(-jnp.abs(v)))


def chunk_terms(info_ref, count, chunk, size, dt_ref, bias_ref, alog_ref, spread):
    first = info_ref[0] + chunk * size
    rows = lax.broadcasted_iota(jnp.int32, (size, size), 0)
    cols = lax.broadcasted_iota(jnp.int32, (size, size), 1)
    seg_row = seg_at(info_ref, count, first + rows)
    seg_col = seg_at(info_ref, count, first + cols)
    seg_one = seg_at(info_ref, count, first + lax.broadcasted_iota(jnp.int32, (size, 1), 0))
    seg_prev = seg_at(info_ref, count, first - 1)
    seg_last = seg_at(info_ref, count, first + size - 1)
    raw = dt_ref.astype(F32) + bias_ref[...]
    delta = softplus(raw)
    decay_rate = -jnp.exp(alog_ref[...])
    rates = delta * decay_rate
    lower = jnp.where(rows >= cols, 1.0, 0.0)
    cum = dot(lower, rates, precision=HIGH)
    upper = jnp.where(rows <= cols, 1.0, 0.0)
    cum_t = dot(rates, upper, TN, precision=HIGH)
    lead = jnp.where(seg_one == seg_prev, jnp.exp(cum), 0.0)
    trail = jnp.where(seg_one == seg_last, jnp.exp(cum[size - 1 :, :] - cum), 0.0)
    same = seg_row == seg_col
    return (rows, cols, same, seg_one, raw, delta, decay_rate, cum, cum_t, lead, trail, upper)


def pair_width(heads, width):
    head = width // heads
    per = max(1, 128 // head)
    while heads % per:
        per -= 1
    return head, per


def flip(index, mask):
    out = index
    bit = 1
    while bit <= mask:
        if mask & bit:
            out = out + bit - 2 * bit * lax.rem(lax.div(index, bit), 2)
        bit *= 2
    return out


def push(src, dst, send, recv, f, c):
    return pltpu.make_async_remote_copy(
        src_ref=src, dst_ref=dst, send_sem=send, recv_sem=recv,
        device_id={"fsdp": f, "context": c}, device_id_type=MESH,
    )


class Gather:
    def __init__(self, spans, ranges, shard, full, item, sems):
        self.f, self.c = lax.axis_index("fsdp"), lax.axis_index("context")
        self.spans, self.ranges, self.shard, self.full, self.item = spans, ranges, shard, full, item
        self.sems = sems
        self.half = shard.shape[0] // 2

    def sem(self, kind, k):
        return self.sems[kind].at[self.item, k]

    def block(self, k, flip_c):
        return self.full.at[flip(self.f, k) * self.ranges + flip(self.c, flip_c)]

    def column(self, k):
        return push(
            self.shard, self.full.at[self.f * self.ranges + self.c],
            self.sem(0, k), self.sem(1, k), flip(self.f, k), self.c,
        )

    def arrived(self, k):
        push(
            self.shard, self.block(k, 0), self.sem(0, k), self.sem(1, k), flip(self.f, k), self.c
        ).wait_recv()

    def side(self, k, way):
        source = self.block(k, 0) if k else self.shard
        return push(
            source, self.block(k, 0), self.sem(2 * way, k), self.sem(2 * way + 1, k),
            self.f, flip(self.c, way),
        )

    def side_arrived(self, k, way):
        block = self.block(k, way)
        push(
            block, block, self.sem(2 * way, k), self.sem(2 * way + 1, k), self.f, flip(self.c, way)
        ).wait_recv()

    def relay(self, k, way):
        other = 3 - way
        part = pl.ds((way - 1) * self.half, self.half)
        block = self.block(k, other).at[part]
        return push(
            block, block, self.sem(4 + 2 * way, k), self.sem(5 + 2 * way, k),
            self.f, flip(self.c, way),
        )

    def relay_arrived(self, k, way):
        part = pl.ds((way - 1) * self.half, self.half)
        block = self.block(k, 3).at[part]
        push(
            block, block, self.sem(4 + 2 * way, k), self.sem(5 + 2 * way, k),
            self.f, flip(self.c, way),
        ).wait_recv()

    def start_columns(self):
        for k in range(1, self.spans):
            self.column(k).start()

    def start_sides(self, k):
        if k:
            self.arrived(k)
        for way in (1, 2):
            self.side(k, way).start()

    def start_relays(self, k):
        for way in (2, 1):
            self.side_arrived(k, 3 - way)
            self.relay(k, way).start()

    def finish(self):
        for k in range(self.spans):
            for way in (1, 2):
                self.relay_arrived(k, way)

    def drain(self):
        for k in range(self.spans):
            if k:
                self.column(k).wait_send()
            for way in (1, 2):
                self.side(k, way).wait_send()
                self.relay(k, way).wait_send()


def forward_kernel(
    count, heads, taps, spans, ranges,
    info_ref, hidden_ref, gain_ref, packed_ref, gate_ref, out_ref, taps_ref, shift_ref,
    bias_ref, alog_ref, spread_ref,
    normed_ref, proj_ref, edge_ref, xact_ref, bc_ref,
    y_ref, full_ref, state_ref, final_ref, packed_all, gate_all, out_all,
    normed, proj, weights, ext, before, carry, total,
    s0, s1, s2, s3, s4, s5, s6, s7, s8, s9, local, edge_sems,
):
    sems = (s0, s1, s2, s3, s4, s5, s6, s7, s8, s9)
    size, width = xact_ref.shape
    states = bc_ref.shape[1] // 2
    step = pl.program_id(0)
    steps = pl.num_programs(0)
    length = hidden_ref.shape[0]
    pad = before.shape[0]
    mixed_width = width + 2 * states
    f, c = lax.axis_index("fsdp"), lax.axis_index("context")
    first = Gather(spans, ranges, packed_ref, weights, 0, sems)
    later = [
        Gather(spans, ranges, gate_ref, gate_all, 1, sems),
        Gather(spans, ranges, out_ref, out_all, 2, sems),
    ]
    own = f * ranges + c
    own_copies = [
        pltpu.make_async_copy(gate_ref, gate_all.at[own], local.at[0]),
        pltpu.make_async_copy(out_ref, out_all.at[own], local.at[1]),
    ]
    keep = pltpu.make_async_copy(weights, packed_all, local.at[2])
    edge_to = push(
        hidden_ref.at[pl.ds(length - pad, pad)], before, edge_sems.at[0], edge_sems.at[1],
        f, lax.rem(c + 1, ranges),
    )
    gain = gain_ref[...]

    def norm(rows):
        wide = rows.astype(F32)
        scale = lax.rsqrt(jnp.mean(wide * wide, axis=1, keepdims=True) + EPSILON)
        return (wide * scale * gain).astype(BF)

    @pl.when(step == 0)
    def _():
        barrier = pltpu.get_barrier_semaphore()
        for k in range(1, spans):
            pl.semaphore_signal(
                barrier, inc=1, device_id={"fsdp": flip(f, k), "context": c}, device_id_type=MESH
            )
        for k in range(1, ranges):
            pl.semaphore_signal(
                barrier, inc=1, device_id={"fsdp": f, "context": lax.rem(c + k, ranges)},
                device_id_type=MESH,
            )
        pl.semaphore_wait(barrier, spans + ranges - 2)
        first.start_sides(0)
        first.start_columns()
        edge_to.start()
        for copy in own_copies:
            copy.start()
        weights[own] = packed_ref[...]
        carry[...] = jnp.zeros_like(carry)
        total[...] = jnp.zeros_like(total)

        @pl.loop(0, steps)
        def _(i):
            at = pl.ds(pl.multiple_of(i * size, size), size)
            normed[at, :] = norm(hidden_ref[at, :])

        for k in range(1, spans):
            first.start_sides(k)
            first.start_relays(k - 1)
        for gather in later:
            gather.start_columns()
        first.start_relays(spans - 1)
        for gather in later:
            gather.start_sides(0)
        edge_to.wait()
        first.finish()
        keep.start()

        @pl.loop(0, length // (2 * size))
        def _(i):
            at = pl.ds(pl.multiple_of(i * 2 * size, 2 * size), 2 * size)
            to = pl.ds(pl.multiple_of(i * 2 * size + pad, pad), 2 * size)
            proj[to, :] = dot(
                normed[at, :], weights[...].reshape(-1, weights.shape[2])
            ).astype(BF)

        head_rows = norm(before[...])
        head_rows = jnp.where(c == 0, jnp.zeros_like(head_rows), head_rows)
        proj[0:pad, :] = dot(head_rows, weights[...].reshape(-1, weights.shape[2])).astype(BF)
        edge_ref[...] = proj[0:pad, :].astype(F32)[pad - 8 :, :]

    for k in range(1, spans):
        @pl.when(step == (k * (length // size)) // spans)
        def _():
            for gather in later:
                gather.start_sides(k)
            for gather in later:
                gather.start_relays(k - 1)

    rows_at = pl.ds(pl.multiple_of(step * size, size), size)
    ext_at = pl.ds(pl.multiple_of(step * size, pad), size + pad)
    normed_ref[...] = normed[rows_at, :]
    proj_ref[...] = proj[pl.ds(pl.multiple_of(step * size + pad, pad), size), :]
    ext[...] = proj[ext_at, :mixed_width].astype(F32)
    position = info_ref[0] + step * size + lax.broadcasted_iota(jnp.int32, (size, mixed_width), 0)
    begin = jnp.zeros_like(position)
    for k in range(1, count):
        begin = jnp.where(position >= info_ref[k], info_ref[k], begin)
    since = position - begin
    pre = ext[pad : pad + size, :] * taps_ref[taps - 1 : taps, :] + shift_ref[...]
    for k in range(1, taps):
        moved = jnp.where(since >= k, ext[pad - k : pad - k + size, :], 0.0)
        pre = pre + moved * taps_ref[taps - 1 - k : taps - k, :]
    act = (pre * jax.nn.sigmoid(pre)).astype(BF)
    xact_ref[...] = act[:, :width]
    bc_ref[...] = act[:, width:]

    spread = spread_ref[...]
    (rows, cols, same, seg_one, raw, delta, decay_rate, cum, cum_t, lead, trail, upper) = (
        chunk_terms(
            info_ref, count, step, size,
            proj_ref[:, mixed_width : mixed_width + heads], bias_ref, alog_ref, spread,
        )
    )
    neg = jnp.where((rows >= cols) & same, 0.0, NEG)
    seg_before = seg_at(info_ref, count, info_ref[0] - 1)
    full_ref[...] = jnp.where(seg_one == seg_before, jnp.exp(cum + total[0:1, :]), 0.0)
    total[0:1, :] = total[0:1, :] + cum[size - 1 :, :]
    x = xact_ref[...].astype(F32)
    xdt = (x * expand(delta, spread)).astype(BF)
    b_rows = bc_ref[:, :states]
    c_rows = bc_ref[:, states:]
    scores = dot(c_rows, b_rows, NT)
    held = carry[...]
    held_b = held.astype(BF)
    state_ref[0] = held_b
    lead_wide = expand(lead, spread)
    y_ref[...] = dot(c_rows, held_b) * lead_wide
    head, per = pair_width(heads, width)
    span = head * per
    lane = lax.broadcasted_iota(jnp.int32, (size, span), 1) // head
    for group in range(heads // per):
        at = slice(group * span, (group + 1) * span)
        xg = xdt[:, at]
        out = None
        for k in range(per):
            h = group * per + k
            decay = jnp.exp(cum[:, h : h + 1] - cum_t[h : h + 1, :] + neg)
            part = dot((decay * scores).astype(BF), xg)
            out = part if out is None else jnp.where(lane >= k, part, out)
        y_ref[:, at] = y_ref[:, at] + out
    weighted = (xdt.astype(F32) * expand(trail, spread)).astype(BF)
    carry[...] = lead_wide[size - 1 :, :] * held + dot(b_rows, weighted, TN)

    @pl.when(step == steps - 1)
    def _():
        final_ref[:states, :] = carry[...]
        final_ref[states:, :] = expand(
            jnp.broadcast_to(full_ref[size - 1 :, :], (8, heads)), spread
        )
        for gather in later:
            gather.start_relays(spans - 1)
        keep.wait()
        for copy in own_copies:
            copy.wait()
        for gather in later:
            gather.finish()
        for gather in [first] + later:
            gather.drain()


def backward_kernel(
    count, heads, info_ref, x_ref, bc_ref, dt_ref, bias_ref, alog_ref, skip_ref, spread_ref,
    y_ref, dy_ref, state_ref, start_ref, in_ref, leave_ref,
    dx_ref, dbc_ref, ddt_ref, sums_ref, carry,
):
    size, width = x_ref.shape
    states = bc_ref.shape[1] // 2
    step = pl.program_id(0)
    chunk = pl.num_programs(0) - 1 - step

    @pl.when(step == 0)
    def _():
        carry[...] = leave_ref[...]
        sums_ref[...] = jnp.zeros_like(sums_ref)

    spread = spread_ref[...]
    (rows, cols, same, seg_one, raw, delta, decay_rate, cum, cum_t, lead, trail, upper) = (
        chunk_terms(info_ref, count, chunk, size, dt_ref[:, :heads], bias_ref, alog_ref, spread)
    )
    neg = jnp.where((rows <= cols) & same, 0.0, NEG)
    x = x_ref[...].astype(F32)
    delta_wide = expand(delta, spread)
    xdt = (x * delta_wide).astype(BF)
    xdt_f = xdt.astype(F32)
    dy = dy_ref[...]
    dy_f = dy.astype(F32)
    b_rows = bc_ref[:, :states]
    c_rows = bc_ref[:, states:]
    scores = dot(b_rows, c_rows, NT)
    grad_state = carry[...]
    grad_state_b = grad_state.astype(BF)
    held = state_ref[0].astype(F32) + expand(start_ref[0], spread)[0:1, :] * in_ref[...]
    held_b = held.astype(BF)
    trail_wide = expand(trail, spread)
    lead_wide = expand(lead, spread)
    state_part = dot(b_rows, grad_state_b) * trail_wide
    dx_ref[...] = state_part
    head, per = pair_width(heads, width)
    span = head * per
    lane = lax.broadcasted_iota(jnp.int32, (size, span), 1) // head
    dscore = jnp.zeros((size, size), F32)
    for group in range(heads // per):
        at = slice(group * span, (group + 1) * span)
        xg = xdt[:, at]
        dyg = dy[:, at]
        out = None
        for k in range(per):
            h = group * per + k
            decay = jnp.exp(cum_t[h : h + 1, :] - cum[:, h : h + 1] + neg)
            part = dot((decay * scores).astype(BF), dyg)
            out = part if out is None else jnp.where(lane >= k, part, out)
            own = jnp.where(lane == k, xg, jnp.zeros_like(xg))
            dscore = dscore + decay * dot(own, dyg, NT)
        dx_ref[:, at] = dx_ref[:, at] + out
    dxdt = dx_ref[...]
    dscore_b = dscore.astype(BF)
    led = (dy_f * lead_wide).astype(BF)
    weighted = (xdt_f * trail_wide).astype(BF)
    dbc_ref[:, :states] = dot(dscore_b, c_rows) + dot(weighted, grad_state_b, NT)
    dbc_ref[:, states:] = dot(dscore_b, b_rows, TN) + dot(led, held_b, NT)
    flows = per_head(dy_f * y_ref[...] - xdt_f * dxdt, spread)
    kept = jnp.sum(xdt_f * state_part, axis=0, keepdims=True) + lead_wide[
        size - 1 :, :
    ] * jnp.sum(held * grad_state, axis=0, keepdims=True)
    at_end = per_head(jnp.broadcast_to(kept, (8, width)), spread)[0:1, :]
    drate = dot(upper, flows, precision=HIGH) + at_end
    ddelta = per_head(x * dxdt, spread) + drate * decay_rate
    draw = ddelta * jax.nn.sigmoid(raw)
    ddt_ref[...] = draw
    skip_sum = per_head(
        jnp.broadcast_to(jnp.sum(dy_f * x, axis=0, keepdims=True), (8, width)), spread
    )[0:1, :]
    sums_ref[0:1, :] += jnp.sum(draw, axis=0, keepdims=True)
    sums_ref[1:2, :] += jnp.sum(drate * delta, axis=0, keepdims=True) * decay_rate
    sums_ref[2:3, :] += skip_sum
    skip_wide = expand(jnp.broadcast_to(skip_ref[...], (8, heads)), spread)[0:1, :]
    dx_ref[...] = dxdt * delta_wide + skip_wide * dy_f
    carry[...] = lead_wide[size - 1 :, :] * grad_state + dot(c_rows, led, TN)


def conv_back_kernel(
    count, taps, info_ref, v_ref, edge_ref, g_ref, w_ref, b_ref,
    out_ref, tail_ref, before_ref, grads_ref, ext, shifted_g,
):
    length, width = v_ref.shape
    first = info_ref[0]
    local = lax.broadcasted_iota(jnp.int32, (length, width), 0)
    ext[0:8, :] = edge_ref[...].astype(F32)
    ext[8 : 8 + length, :] = v_ref[...].astype(F32)
    pre = jnp.zeros((length, width), F32) + b_ref[...]
    begin = jnp.zeros_like(local)
    for k in range(1, count):
        begin = jnp.where(first + local >= info_ref[k], info_ref[k], begin)
    since = first + local - begin
    for k in range(taps):
        moved = ext[8 - k : 8 - k + length, :]
        if k:
            moved = jnp.where(since >= k, moved, 0.0)
        pre = pre + moved * w_ref[taps - 1 - k : taps - k, :]
    sig = jax.nn.sigmoid(pre)
    grad = g_ref[...].astype(F32) * sig * (1.0 + pre * (1.0 - sig))
    grads_ref[...] = jnp.zeros_like(grads_ref)
    grads_ref[taps : taps + 1, :] = jnp.sum(grad, axis=0, keepdims=True)
    back = jnp.zeros((length, width), F32)
    early = jnp.zeros((8, width), F32)
    shifted_g[0:8, :] = jnp.zeros((8, width), F32)
    shifted_g[8 + length :, :] = jnp.zeros((8, width), F32)
    for k in range(taps):
        kept = grad
        if k:
            kept = jnp.where(since >= k, grad, 0.0)
        moved = ext[8 - k : 8 - k + length, :]
        at = taps - 1 - k
        grads_ref[at : at + 1, :] = jnp.sum(kept * moved, axis=0, keepdims=True)
        shifted_g[8 : 8 + length, :] = kept
        weight = w_ref[at : at + 1, :]
        back = back + shifted_g[8 + k : 8 + k + length, :] * weight
        early = early + shifted_g[k : k + 8, :] * weight
    out_ref[...] = back.astype(BF)
    tail_ref[...] = back[length - 8 :, :]
    before_ref[...] = early


def whole(shape):
    return pl.BlockSpec(shape, lambda i: (0,) * len(shape))


SMEM = pl.BlockSpec(memory_space=pltpu.SMEM)


def conv_back(info, count, values, edge, grad, weight, shift, offset):
    length, width = grad.shape
    taps = weight.shape[0]
    block = 128
    col = lambda r: pl.BlockSpec((r, block), lambda i: (0, i))
    shifted_col = lambda r: pl.BlockSpec((r, block), lambda i: (0, i + offset // block))
    return pl.pallas_call(
        functools.partial(conv_back_kernel, count, taps),
        grid=(width // block,),
        in_specs=[SMEM, shifted_col(length), shifted_col(8), col(length), col(taps), col(1)],
        out_specs=[col(length), col(8), col(8), col(8)],
        out_shape=[
            jax.ShapeDtypeStruct((length, width), BF),
            jax.ShapeDtypeStruct((8, width), F32),
            jax.ShapeDtypeStruct((8, width), F32),
            jax.ShapeDtypeStruct((8, width), F32),
        ],
        scratch_shapes=[pltpu.VMEM((length + 8, block), F32), pltpu.VMEM((length + 16, block), F32)],
        name="conv_back",
    )(info, values, edge, grad, weight, shift)


def forward(info, count, hidden, gain, packed, gate, out, taps, shift, bias, alog, spread):
    length, model = hidden.shape
    heads, width = spread.shape
    states = (taps.shape[1] - width) // 2
    spans, ranges = lax.axis_size("fsdp"), lax.axis_size("context")
    chunks = length // CHUNK
    wide = packed.shape[1]
    pad = 16
    row = lambda c: pl.BlockSpec((CHUNK, c), lambda i: (i, 0))
    anywhere = pl.BlockSpec(memory_space=pl.ANY)
    gathered = lambda v: jax.ShapeDtypeStruct((spans * ranges,) + v.shape, v.dtype)
    sem = pltpu.SemaphoreType.DMA((3, spans))
    return pl.pallas_call(
        functools.partial(forward_kernel, count, heads, taps.shape[0], spans, ranges),
        grid=(chunks,),
        in_specs=[
            SMEM, whole((length, model)), whole((1, model)), whole(packed.shape),
            whole(gate.shape), whole(out.shape), whole(taps.shape), whole((1, taps.shape[1])),
            whole((1, heads)), whole((1, heads)), whole((heads, width)),
        ],
        out_specs=[
            row(model), row(wide), whole((8, wide)), row(width), row(2 * states),
            row(width), row(heads),
            pl.BlockSpec((1, states, width), lambda i: (i, 0, 0)), whole((states + 8, width)),
            anywhere, anywhere, anywhere,
        ],
        out_shape=[
            jax.ShapeDtypeStruct((length, model), BF),
            jax.ShapeDtypeStruct((length, wide), BF),
            jax.ShapeDtypeStruct((8, wide), F32),
            jax.ShapeDtypeStruct((length, width), BF),
            jax.ShapeDtypeStruct((length, 2 * states), BF),
            jax.ShapeDtypeStruct((length, width), F32),
            jax.ShapeDtypeStruct((length, heads), F32),
            jax.ShapeDtypeStruct((chunks, states, width), BF),
            jax.ShapeDtypeStruct((states + 8, width), F32),
            gathered(packed), gathered(gate), gathered(out),
        ],
        scratch_shapes=[
            pltpu.VMEM((length, model), BF),
            pltpu.VMEM((length + pad, wide), BF),
            pltpu.VMEM((spans * ranges,) + packed.shape, BF),
            pltpu.VMEM((CHUNK + pad, width + 2 * states), F32),
            pltpu.VMEM((pad, model), BF),
            pltpu.VMEM((states, width), F32),
            pltpu.VMEM((8, heads), F32),
        ] + [sem] * 10 + [pltpu.SemaphoreType.DMA((3,)), pltpu.SemaphoreType.DMA((2,))],
        compiler_params=pltpu.CompilerParams(collective_id=0, has_side_effects=True),
        name="forward",
    )(info, hidden, gain, packed, gate, out, taps, shift, bias, alog, spread)


def scan_backward(info, count, x, bc, proj, bias, alog, skip, spread, y, dy, states_at, start, state_in, leaving):
    length, width = x.shape
    heads = bias.shape[1]
    states = bc.shape[1] // 2
    dt_block = (width + 2 * states) // 128
    chunks = length // CHUNK
    row = lambda c: pl.BlockSpec((CHUNK, c), lambda i: (chunks - 1 - i, 0))
    return pl.pallas_call(
        functools.partial(backward_kernel, count, heads),
        grid=(chunks,),
        in_specs=[
            SMEM, row(width), row(2 * states),
            pl.BlockSpec((CHUNK, 128), lambda i: (chunks - 1 - i, dt_block)),
            whole((1, heads)), whole((1, heads)), whole((1, heads)), whole((heads, width)),
            row(width), row(width),
            pl.BlockSpec((1, states, width), lambda i: (chunks - 1 - i, 0, 0)),
            pl.BlockSpec((1, 8, heads), lambda i: (chunks - 1 - i, 0, 0)),
            whole((states, width)), whole((states, width)),
        ],
        out_specs=[row(width), row(2 * states), row(heads), whole((8, heads))],
        out_shape=[
            jax.ShapeDtypeStruct((length, width), F32),
            jax.ShapeDtypeStruct((length, 2 * states), F32),
            jax.ShapeDtypeStruct((length, heads), F32),
            jax.ShapeDtypeStruct((8, heads), F32),
        ],
        scratch_shapes=[pltpu.VMEM((states, width), F32)],
        name="scan_backward",
    )(info, x, bc, proj, bias, alog, skip, spread, y, dy, states_at, start, state_in, leaving)


def ring(axis, step):
    count = lax.axis_size(axis)
    return [(source, (source + step) % count) for source in range(count)]


def shifted(value, axis, steps):
    count = lax.axis_size(axis)
    initial, last = (max(0, -steps), min(count, count - steps))
    return lax.ppermute(value, axis, [(source, source + steps) for source in range(initial, last)])


def total_over(value, axis):
    if lax.axis_size(axis) == 2:
        return value.astype(F32) + lax.ppermute(value, axis, ring(axis, 1)).astype(F32)
    return jnp.sum(gather_axis(value, axis, 0).astype(F32), axis=0)


def share_over(value, axis, dim):
    count, index = (lax.axis_size(axis), lax.axis_index(axis))
    size = value.shape[dim] // count
    part = lambda at: lax.dynamic_slice_in_dim(value, at * size, size, dim)
    result = part(index).astype(F32)
    for step in range(1, count):
        sent = part((index + step) % count)
        result = result + lax.ppermute(sent, axis, ring(axis, step)).astype(F32)
    return result


def gather_axis(value, axis, dim):
    count, index = (lax.axis_size(axis), lax.axis_index(axis))
    shape = value.shape[:dim] + (count,) + value.shape[dim:]
    result = lax.dynamic_update_index_in_dim(jnp.zeros(shape, value.dtype), value, index, dim)
    for step in range(1, count):
        got = lax.ppermute(value, axis, ring(axis, step))
        result = lax.dynamic_update_index_in_dim(result, got, (index - step) % count, dim)
    return result


def columns(value, widths):
    pieces, at = ([], 0)
    for width in widths:
        pieces.append(value[..., at : at + width])
        at += width
    return pieces


def scatter_axis(values, axis, dim):
    count, index = (lax.axis_size(axis), lax.axis_index(axis))
    part = lambda at: jnp.concatenate(
        [lax.dynamic_index_in_dim(value, at, dim, False) for value in values], axis=-1
    )
    received = [
        lax.ppermute(part((index + step) % count), axis, ring(axis, step))
        for step in range(1, count)
    ]
    result = part(index).astype(F32)
    for got in received:
        result = result + got.astype(F32)
    return result


def scatter_first(values):
    fsdp, context = (lax.axis_size("fsdp"), lax.axis_size("context"))
    shaped = [v.astype(BF).reshape(fsdp, context, -1, v.shape[-1]) for v in values]
    return scatter_axis(shaped, "context", 1).astype(BF)


def scatter_second(half, values):
    return columns(scatter_axis([half], "fsdp", 0), [v.shape[-1] for v in values])


def chain(state, decay_rows, direction):
    states = state.shape[0]
    packed = jnp.concatenate([state, decay_rows], axis=0).astype(BF)
    total = jnp.zeros_like(state)
    factor = jnp.ones((1, state.shape[1]), F32)
    for step in range(1, lax.axis_size("context")):
        got = shifted(packed, "context", direction * step).astype(F32)
        total = total + factor * got[:states]
        factor = factor * got[states : states + 1]
    return total


def body(
    hidden, d_mixed, seq_lengths, norm_gain, w_gate, w_x, w_bc, w_dt, conv_x, conv_x_bias,
    conv_bc, conv_bc_bias, dt_bias, a_log, d_skip, gate_gain, w_out,
):
    row_count, model_width = hidden.shape
    lanes = lax.axis_size("tensor")
    lane = lax.axis_index("tensor")
    share_width = model_width // lanes
    share_start = lane * share_width
    inner_local = conv_x.shape[1]
    inner_width = inner_local * lanes
    heads = dt_bias.shape[0]
    bc_width = conv_bc.shape[1]
    bc_cols = bc_width // lanes
    states = bc_width // 2
    lengths = seq_lengths[0]
    count = lengths.shape[0]
    first_row = lax.axis_index("context") * row_count
    starts = (jnp.cumsum(lengths) - lengths).astype(jnp.int32)
    info = jnp.concatenate([first_row.astype(jnp.int32)[None], starts[1:]])
    spread = (
        lax.broadcasted_iota(jnp.int32, (heads, inner_local), 1) // (inner_local // heads)
        == lax.broadcasted_iota(jnp.int32, (heads, inner_local), 0)
    ).astype(BF)

    widened = hidden.astype(F32)
    row_scale = lax.rsqrt(jnp.mean(widened * widened, axis=1, keepdims=True) + EPSILON)
    mixed_width = inner_local + bc_width
    spare = -(-heads // 128) * 128 - heads
    packed = jnp.concatenate(
        [w_x, w_bc, w_dt, jnp.zeros((w_x.shape[0], spare), w_x.dtype)], axis=1
    )
    bias_row, alog_row, skip_row = (dt_bias[None, :], a_log[None, :], d_skip[None, :])
    (
        normed, proj, edge, x_act, bc_act, y_local, full, states_at, final,
        packed_weight, gate_weight, out_weight,
    ) = forward(
        info, count, hidden, norm_gain[None, :], packed, w_gate, w_out.T,
        jnp.concatenate([conv_x, conv_bc], axis=1),
        jnp.concatenate([conv_x_bias, conv_bc_bias])[None, :],
        bias_row, alog_row, spread,
    )
    packed_weight = packed_weight.reshape(model_width, -1)
    gate_weight = gate_weight.reshape(model_width, -1)
    out_weight = out_weight.reshape(model_width, -1)
    x_weight = packed_weight[:, :inner_local]
    side_weight = packed_weight[:, inner_local : mixed_width + heads]
    z_proj = dot(normed, gate_weight).astype(BF)
    decay_rows = final[states:]
    state_in = chain(final[:states], decay_rows, 1)
    c_rows = bc_act[:, states:]
    full_wide = expand(full, spread)
    y = y_local + dot(c_rows, state_in.astype(BF)) * full_wide
    skip_wide = jnp.repeat(d_skip, inner_local // heads)[None, :]
    y_full = y + skip_wide * x_act.astype(F32)
    z = z_proj.astype(F32)
    sig = jax.nn.sigmoid(z)
    gate = z * sig
    gated = y_full * gate
    grad_norm_out = dot(d_mixed, out_weight)
    scaled = grad_norm_out * gate_gain[None, :]
    both = total_over(
        jnp.stack([jnp.sum(gated * gated, axis=1), jnp.sum(scaled * gated, axis=1)]), "tensor"
    )
    gate_scale = lax.rsqrt(both[0][:, None] / inner_width + EPSILON)
    unit = gated * gate_scale
    normed_out = (unit * gate_gain[None, :]).astype(BF)
    grad_gated = gate_scale * scaled - gated * gate_scale**3 * (both[1][:, None] / inner_width)
    dy = (grad_gated * gate).astype(BF)
    grad_zb = (grad_gated * y_full * sig * (1.0 + z * (1.0 - sig))).astype(BF)
    gain_term = jnp.sum(grad_norm_out * unit, axis=0)
    grad_in = dot(c_rows, (dy.astype(F32) * full_wide).astype(BF), TN)
    leaving = chain(grad_in, decay_rows, -1)
    out_partial = dot(normed_out, out_weight, NT).astype(BF)
    out_term = dot(d_mixed, normed_out, TN).astype(BF)
    gate_term = dot(normed, grad_zb, TN).astype(BF)
    leaving, out_partial, out_term, gate_term = lax.optimization_barrier(
        (leaving, out_partial, out_term, gate_term)
    )
    mixed_share = share_over(out_partial, "tensor", 1)
    hidden_share = lax.dynamic_slice_in_dim(widened, share_start, share_width, 1)
    mixed = (hidden_share + mixed_share).astype(BF)
    early_half = scatter_first([out_term, gate_term])
    starting = jnp.concatenate([jnp.ones((1, heads), F32), full[CHUNK - 1 :: CHUNK][:-1]], axis=0)
    starting = jnp.broadcast_to(starting[:, None, :], (starting.shape[0], 8, heads))
    dx_act, dbc_act, ddt, head_sums = scan_backward(
        info, count, x_act, bc_act, proj, bias_row, alog_row, skip_row, spread, y, dy,
        states_at, starting, state_in, leaving,
    )
    dx_act, dbc_act, early_half = lax.optimization_barrier((dx_act, dbc_act, early_half))
    grad_w_out, grad_w_gate = scatter_second(early_half, [out_term, gate_term])
    grad_w_out = grad_w_out.T
    dbc_all = total_over(dbc_act.astype(BF), "tensor")
    dx_b, x_tail, x_before, x_grads = conv_back(
        info, count, proj, edge, dx_act, conv_x, conv_x_bias[None, :], 0
    )
    dbc_b, bc_tail, bc_before, bc_grads = conv_back(
        info, count, proj, edge, dbc_all, conv_bc, conv_bc_bias[None, :], inner_local
    )
    x_next = shifted(x_before, "context", -1)
    bc_next = shifted(bc_before, "context", -1)
    dx_b = lax.dynamic_update_slice(dx_b, (x_tail + x_next).astype(BF), (row_count - 8, 0))
    dbc_b = lax.dynamic_update_slice(dbc_b, (bc_tail + bc_next).astype(BF), (row_count - 8, 0))
    ddt_b = ddt.astype(BF)
    side_b = jnp.concatenate([dbc_b, ddt_b], axis=1)
    late = [dot(normed, dx_b, TN), dot(normed, side_b, TN)]
    grad_w_x, grad_side = scatter_second(scatter_first(late), late)
    grad_normed = dot(grad_zb, gate_weight, NT) + dot(dx_b, x_weight, NT)
    dbc_own = lax.dynamic_slice_in_dim(dbc_b, lane * bc_cols, bc_cols, 1)
    bc_weight_own = lax.dynamic_slice_in_dim(side_weight, lane * bc_cols, bc_cols, 1)
    grad_normed = grad_normed + dot(dbc_own, bc_weight_own, NT)
    grad_normed = grad_normed + dot(ddt_b, side_weight[:, bc_width:], NT)
    grad_share = share_over(grad_normed.astype(BF), "tensor", 1)
    gain_share = lax.dynamic_slice_in_dim(norm_gain, share_start, share_width, 0)
    norm_term = jnp.sum(grad_share * hidden_share * row_scale, axis=0)
    gained = grad_share * gain_share[None, :]
    dot_rows = total_over(jnp.sum(gained * hidden_share, axis=1), "tensor")
    dot_rows = dot_rows[:, None] / model_width
    dmix_share = lax.dynamic_slice_in_dim(d_mixed, share_start, share_width, 1)
    grad_hidden = (
        dmix_share.astype(F32) + row_scale * gained - hidden_share * row_scale**3 * dot_rows
    )
    taps = conv_x.shape[0]
    pieces = [
        x_grads[: taps + 1], bc_grads[: taps + 1], head_sums[:3], gain_term, norm_term,
    ]
    flat = jnp.concatenate([p.reshape(-1) for p in pieces])
    padded = -(-flat.shape[0] // 1024) * 1024
    flat = jnp.concatenate([flat, jnp.zeros((padded - flat.shape[0],), F32)]).reshape(-1, 128)
    flat = total_over(total_over(flat, "context"), "fsdp").reshape(-1)
    summed, at = ([], 0)
    for p in pieces:
        size = p.size
        summed.append(flat[at : at + size].reshape(p.shape))
        at += size
    sx, sbc, sh, sgain, snorm = summed
    return (
        mixed, grad_hidden, snorm, grad_w_gate, grad_w_x, grad_side[:, :bc_width],
        grad_side[:, bc_width:], sx[:taps], sx[taps], sbc[:taps], sbc[taps],
        sh[0], sh[1], sh[2], sgain, grad_w_out,
    )


def solution(mesh):
    return jax.shard_map(
        body,
        mesh=mesh,
        in_specs=(
            P(("fsdp", "context"), None),
            P(("fsdp", "context"), None),
            P("fsdp", None),
            P(),
            P(("fsdp", "context"), "tensor"),
            P(("fsdp", "context"), "tensor"),
            P(("fsdp", "context"), None),
            P(("fsdp", "context"), "tensor"),
            P(None, "tensor"),
            P("tensor"),
            P(),
            P(),
            P("tensor"),
            P("tensor"),
            P("tensor"),
            P("tensor"),
            P("tensor", ("fsdp", "context")),
        ),
        out_specs=(
            P(("fsdp", "context"), "tensor"),
            P(("fsdp", "context"), "tensor"),
            P("tensor"),
            P(("fsdp", "context"), "tensor"),
            P(("fsdp", "context"), "tensor"),
            P(("fsdp", "context"), None),
            P(("fsdp", "context"), "tensor"),
            P(None, "tensor"),
            P("tensor"),
            P(),
            P(),
            P("tensor"),
            P("tensor"),
            P("tensor"),
            P("tensor"),
            P("tensor", ("fsdp", "context")),
        ),
        check_vma=False,
    )
```

```python
import functools
import jax
import jax.numpy as jnp
from jax import lax
from jax.experimental import pallas as pl
from jax.experimental.pallas import tpu as pltpu
from jax.sharding import PartitionSpec as P

EPSILON = 1e-05
HIGH = lax.Precision.HIGHEST
BF = jnp.bfloat16
F32 = jnp.float32
CHUNK = 128
NEG = -1e30
MESH = pl.DeviceIdType.MESH
NT = (((1,), (1,)), ((), ()))
TN = (((0,), (0,)), ((), ()))


def dot(a, b, dims=(((1,), (0,)), ((), ())), precision=None):
    return lax.dot_general(a, b, dims, precision=precision, preferred_element_type=F32)


def split2(value):
    high = value.astype(BF)
    return high, (value - high.astype(F32)).astype(BF)


def expand(value, spread):
    high, low = split2(value)
    return dot(high, spread) + dot(low, spread)


def per_head(value, spread):
    high, low = split2(value)
    return dot(high, spread, NT) + dot(low, spread, NT)


def seg_at(info_ref, count, positions):
    found = jnp.where(positions < 0, -1, 0)
    for k in range(1, count):
        found = found + jnp.where(positions >= info_ref[k], 1, 0)
    return found


def softplus(v):
    return jnp.maximum(v, 0.0) + jnp.log1p(jnp.exp(-jnp.abs(v)))


def chunk_terms(info_ref, count, chunk, size, dt_ref, bias_ref, alog_ref, spread):
    first = info_ref[0] + chunk * size
    rows = lax.broadcasted_iota(jnp.int32, (size, size), 0)
    cols = lax.broadcasted_iota(jnp.int32, (size, size), 1)
    seg_row = seg_at(info_ref, count, first + rows)
    seg_col = seg_at(info_ref, count, first + cols)
    seg_one = seg_at(info_ref, count, first + lax.broadcasted_iota(jnp.int32, (size, 1), 0))
    seg_prev = seg_at(info_ref, count, first - 1)
    seg_last = seg_at(info_ref, count, first + size - 1)
    raw = dt_ref.astype(F32) + bias_ref[...]
    delta = softplus(raw)
    decay_rate = -jnp.exp(alog_ref[...])
    rates = delta * decay_rate
    lower = jnp.where(rows >= cols, 1.0, 0.0)
    cum = dot(lower, rates, precision=HIGH)
    upper = jnp.where(rows <= cols, 1.0, 0.0)
    cum_t = dot(rates, upper, TN, precision=HIGH)
    lead = jnp.where(seg_one == seg_prev, jnp.exp(cum), 0.0)
    trail = jnp.where(seg_one == seg_last, jnp.exp(cum[size - 1 :, :] - cum), 0.0)
    same = seg_row == seg_col
    return (rows, cols, same, seg_one, raw, delta, decay_rate, cum, cum_t, lead, trail, upper)


def pair_width(heads, width):
    head = width // heads
    per = max(1, 128 // head)
    while heads % per:
        per -= 1
    return head, per


def flip(index, mask):
    out = index
    bit = 1
    while bit <= mask:
        if mask & bit:
            out = out + bit - 2 * bit * lax.rem(lax.div(index, bit), 2)
        bit *= 2
    return out


def push(src, dst, send, recv, f, c):
    return pltpu.make_async_remote_copy(
        src_ref=src, dst_ref=dst, send_sem=send, recv_sem=recv,
        device_id={"fsdp": f, "context": c}, device_id_type=MESH,
    )


class Gather:
    def __init__(self, spans, ranges, shard, full, item, sems):
        self.f, self.c = lax.axis_index("fsdp"), lax.axis_index("context")
        self.spans, self.ranges, self.shard, self.full, self.item = spans, ranges, shard, full, item
        self.sems = sems
        self.half = shard.shape[0] // 2

    def sem(self, kind, k):
        return self.sems[kind].at[self.item, k]

    def block(self, k, flip_c):
        return self.full.at[flip(self.f, k) * self.ranges + flip(self.c, flip_c)]

    def column(self, k):
        return push(
            self.shard, self.full.at[self.f * self.ranges + self.c],
            self.sem(0, k), self.sem(1, k), flip(self.f, k), self.c,
        )

    def arrived(self, k):
        push(
            self.shard, self.block(k, 0), self.sem(0, k), self.sem(1, k), flip(self.f, k), self.c
        ).wait_recv()

    def side(self, k, way):
        source = self.block(k, 0) if k else self.shard
        return push(
            source, self.block(k, 0), self.sem(2 * way, k), self.sem(2 * way + 1, k),
            self.f, flip(self.c, way),
        )

    def side_arrived(self, k, way):
        block = self.block(k, way)
        push(
            block, block, self.sem(2 * way, k), self.sem(2 * way + 1, k), self.f, flip(self.c, way)
        ).wait_recv()

    def relay(self, k, way):
        other = 3 - way
        part = pl.ds((way - 1) * self.half, self.half)
        block = self.block(k, other).at[part]
        return push(
            block, block, self.sem(4 + 2 * way, k), self.sem(5 + 2 * way, k),
            self.f, flip(self.c, way),
        )

    def relay_arrived(self, k, way):
        part = pl.ds((way - 1) * self.half, self.half)
        block = self.block(k, 3).at[part]
        push(
            block, block, self.sem(4 + 2 * way, k), self.sem(5 + 2 * way, k),
            self.f, flip(self.c, way),
        ).wait_recv()

    def start_columns(self):
        for k in range(1, self.spans):
            self.column(k).start()

    def start_sides(self, k):
        if k:
            self.arrived(k)
        for way in (1, 2):
            self.side(k, way).start()

    def start_relays(self, k):
        for way in (2, 1):
            self.side_arrived(k, 3 - way)
            self.relay(k, way).start()

    def finish(self):
        for k in range(self.spans):
            for way in (1, 2):
                self.relay_arrived(k, way)

    def drain(self):
        for k in range(self.spans):
            if k:
                self.column(k).wait_send()
            for way in (1, 2):
                self.side(k, way).wait_send()
                self.relay(k, way).wait_send()


def forward_kernel(
    count, heads, taps, spans, ranges,
    info_ref, hidden_ref, gain_ref, packed_ref, gate_ref, out_ref, taps_ref, shift_ref,
    bias_ref, alog_ref, spread_ref,
    normed_ref, proj_ref, edge_ref, xact_ref, bc_ref, slope_ref,
    y_ref, full_ref, state_ref, final_ref, packed_all, gate_all, out_all,
    normed, proj, weights, ext, before, carry, total,
    s0, s1, s2, s3, s4, s5, s6, s7, s8, s9, local, edge_sems,
):
    sems = (s0, s1, s2, s3, s4, s5, s6, s7, s8, s9)
    size, width = xact_ref.shape
    states = bc_ref.shape[1] // 2
    step = pl.program_id(0)
    steps = pl.num_programs(0)
    length = hidden_ref.shape[0]
    pad = before.shape[0]
    mixed_width = width + 2 * states
    f, c = lax.axis_index("fsdp"), lax.axis_index("context")
    first = Gather(spans, ranges, packed_ref, weights, 0, sems)
    later = [
        Gather(spans, ranges, gate_ref, gate_all, 1, sems),
        Gather(spans, ranges, out_ref, out_all, 2, sems),
    ]
    own = f * ranges + c
    own_copies = [
        pltpu.make_async_copy(gate_ref, gate_all.at[own], local.at[0]),
        pltpu.make_async_copy(out_ref, out_all.at[own], local.at[1]),
    ]
    keep = pltpu.make_async_copy(weights, packed_all, local.at[2])
    edge_to = push(
        hidden_ref.at[pl.ds(length - pad, pad)], before, edge_sems.at[0], edge_sems.at[1],
        f, lax.rem(c + 1, ranges),
    )
    gain = gain_ref[...]

    def norm(rows):
        wide = rows.astype(F32)
        scale = lax.rsqrt(jnp.mean(wide * wide, axis=1, keepdims=True) + EPSILON)
        return (wide * scale * gain).astype(BF)

    @pl.when(step == 0)
    def _():
        greet(spans, ranges)
        first.start_sides(0)
        first.start_columns()
        edge_to.start()
        for copy in own_copies:
            copy.start()
        weights[own] = packed_ref[...]
        carry[...] = jnp.zeros_like(carry)
        total[...] = jnp.zeros_like(total)

        @pl.loop(0, steps)
        def _(i):
            at = pl.ds(pl.multiple_of(i * size, size), size)
            normed[at, :] = norm(hidden_ref[at, :])

        for k in range(1, spans):
            first.start_sides(k)
            first.start_relays(k - 1)
        for gather in later:
            gather.start_columns()
        first.start_relays(spans - 1)
        for gather in later:
            gather.start_sides(0)
        edge_to.wait()
        first.finish()
        keep.start()

        @pl.loop(0, length // (2 * size))
        def _(i):
            at = pl.ds(pl.multiple_of(i * 2 * size, 2 * size), 2 * size)
            to = pl.ds(pl.multiple_of(i * 2 * size + pad, pad), 2 * size)
            proj[to, :] = dot(
                normed[at, :], weights[...].reshape(-1, weights.shape[2])
            ).astype(BF)

        head_rows = norm(before[...])
        head_rows = jnp.where(c == 0, jnp.zeros_like(head_rows), head_rows)
        proj[0:pad, :] = dot(head_rows, weights[...].reshape(-1, weights.shape[2])).astype(BF)
        edge_ref[...] = proj[0:pad, :].astype(F32)[pad - 8 :, :]

    for k in range(1, spans):
        @pl.when(step == (k * (length // size)) // spans)
        def _():
            for gather in later:
                gather.start_sides(k)
            for gather in later:
                gather.start_relays(k - 1)

    rows_at = pl.ds(pl.multiple_of(step * size, size), size)
    ext_at = pl.ds(pl.multiple_of(step * size, pad), size + pad)
    normed_ref[...] = normed[rows_at, :]
    proj_ref[...] = proj[pl.ds(pl.multiple_of(step * size + pad, pad), size), :]
    ext[...] = proj[ext_at, :mixed_width].astype(F32)
    position = info_ref[0] + step * size + lax.broadcasted_iota(jnp.int32, (size, mixed_width), 0)
    begin = jnp.zeros_like(position)
    for k in range(1, count):
        begin = jnp.where(position >= info_ref[k], info_ref[k], begin)
    since = position - begin
    pre = ext[pad : pad + size, :] * taps_ref[taps - 1 : taps, :] + shift_ref[...]
    for k in range(1, taps):
        moved = jnp.where(since >= k, ext[pad - k : pad - k + size, :], 0.0)
        pre = pre + moved * taps_ref[taps - 1 - k : taps - k, :]
    sig = jax.nn.sigmoid(pre)
    act = (pre * sig).astype(BF)
    slope_ref[...] = (sig * (1.0 + pre * (1.0 - sig))).astype(BF)
    xact_ref[...] = act[:, :width]
    bc_ref[...] = act[:, width:]

    spread = spread_ref[...]
    (rows, cols, same, seg_one, raw, delta, decay_rate, cum, cum_t, lead, trail, upper) = (
        chunk_terms(
            info_ref, count, step, size,
            proj_ref[:, mixed_width : mixed_width + heads], bias_ref, alog_ref, spread,
        )
    )
    neg = jnp.where((rows >= cols) & same, 0.0, NEG)
    seg_before = seg_at(info_ref, count, info_ref[0] - 1)
    full_ref[...] = jnp.where(seg_one == seg_before, jnp.exp(cum + total[0:1, :]), 0.0)
    total[0:1, :] = total[0:1, :] + cum[size - 1 :, :]
    x = xact_ref[...].astype(F32)
    xdt = (x * expand(delta, spread)).astype(BF)
    b_rows = bc_ref[:, :states]
    c_rows = bc_ref[:, states:]
    scores = dot(c_rows, b_rows, NT)
    held = carry[...]
    held_b = held.astype(BF)
    state_ref[0] = held_b
    lead_wide = expand(lead, spread)
    y_ref[...] = dot(c_rows, held_b) * lead_wide
    head, per = pair_width(heads, width)
    span = head * per
    lane = lax.broadcasted_iota(jnp.int32, (size, span), 1) // head
    for group in range(heads // per):
        at = slice(group * span, (group + 1) * span)
        xg = xdt[:, at]
        out = None
        for k in range(per):
            h = group * per + k
            decay = jnp.exp(cum[:, h : h + 1] - cum_t[h : h + 1, :] + neg)
            part = dot((decay * scores).astype(BF), xg)
            out = part if out is None else jnp.where(lane >= k, part, out)
        y_ref[:, at] = y_ref[:, at] + out
    weighted = (xdt.astype(F32) * expand(trail, spread)).astype(BF)
    carry[...] = lead_wide[size - 1 :, :] * held + dot(b_rows, weighted, TN)

    @pl.when(step == steps - 1)
    def _():
        final_ref[:states, :] = carry[...]
        final_ref[states:, :] = expand(
            jnp.broadcast_to(full_ref[size - 1 :, :], (8, heads)), spread
        )
        for gather in later:
            gather.start_relays(spans - 1)
        keep.wait()
        for copy in own_copies:
            copy.wait()
        for gather in later:
            gather.finish()
        for gather in [first] + later:
            gather.drain()


class Scatter:
    def __init__(self, spans, ranges, item, src, half_in, full_in, full_out, far_out, far_in, sems):
        self.f, self.c = lax.axis_index("fsdp"), lax.axis_index("context")
        self.spans, self.ranges, self.item, self.src = spans, ranges, item, src
        self.half_in, self.full_in, self.full_out = half_in, full_in, full_out
        self.far_out, self.far_in, self.sems = far_out, far_in, sems
        self.half = src.shape[1] // 2

    def sem(self, kind, k):
        return self.sems[kind].at[self.item, k]

    def at(self, k, flip_c):
        return flip(self.f, k) * self.ranges + flip(self.c, flip_c)

    def part(self, way):
        return pl.ds((way - 1) * self.half, self.half)

    def half_copy(self, k, way):
        return push(
            self.src.at[self.at(k, 3), self.part(way)], self.half_in.at[way - 1, k],
            self.sem(2 * way - 2, k), self.sem(2 * way - 1, k), self.f, flip(self.c, way),
        )

    def full_copy(self, k, way):
        return push(
            self.full_out.at[way - 1, k], self.full_in.at[way - 1, k],
            self.sem(2 * way + 2, k), self.sem(2 * way + 3, k), self.f, flip(self.c, way),
        )

    def far_copy(self, k):
        return push(
            self.far_out.at[k], self.far_in.at[k], self.sem(8, k), self.sem(9, k),
            flip(self.f, k), self.c,
        )

    def start_halves(self, k):
        for way in (1, 2):
            self.half_copy(k, way).start()

    def start_fulls(self, k):
        for way in (1, 2):
            other = 3 - way
            self.half_copy(k, way).wait_recv()
            index, part, rest = self.at(k, other), self.part(way), self.part(other)
            self.full_out[other - 1, k, part, :] = (
                self.src[index, part, :].astype(F32) + self.half_in[way - 1, k].astype(F32)
            ).astype(BF)
            self.full_out[other - 1, k, rest, :] = self.src[index, rest, :]
            self.full_copy(k, other).start()

    def start_far(self, k, result):
        for way in (1, 2):
            self.full_copy(k, way).wait_recv()
        total = self.src[self.at(k, 0)].astype(F32) + (
            self.full_in[0, k].astype(F32) + self.full_in[1, k].astype(F32)
        )
        if k:
            self.far_out[k] = total.astype(BF)
            self.far_copy(k).start()
        else:
            result[...] = total

    def finish(self, result):
        for k in range(1, self.spans):
            self.far_copy(k).wait_recv()
            result[...] += self.far_in[k].astype(F32)

    def drain(self):
        for k in range(self.spans):
            for way in (1, 2):
                self.half_copy(k, way).wait_send()
                self.full_copy(k, way).wait_send()
            if k:
                self.far_copy(k).wait_send()


def scatter_scratch(spans, items, rows, width):
    return [
        pltpu.VMEM((items, 2, spans, rows // 2, width), BF),
        pltpu.VMEM((items, 2, spans, rows, width), BF),
        pltpu.VMEM((items, 2, spans, rows, width), BF),
        pltpu.VMEM((items, spans, rows, width), BF),
        pltpu.VMEM((items, spans, rows, width), BF),
    ] + [pltpu.SemaphoreType.DMA((items, spans))] * 10


def greet(spans, ranges):
    f, c = lax.axis_index("fsdp"), lax.axis_index("context")
    barrier = pltpu.get_barrier_semaphore()
    for k in range(1, spans):
        pl.semaphore_signal(
            barrier, inc=1, device_id={"fsdp": flip(f, k), "context": c}, device_id_type=MESH
        )
    for k in range(1, ranges):
        pl.semaphore_signal(
            barrier, inc=1, device_id={"fsdp": f, "context": lax.rem(c + k, ranges)},
            device_id_type=MESH,
        )
    pl.semaphore_wait(barrier, spans + ranges - 2)


def backward_kernel(
    count, heads, taps, spans, ranges,
    info_ref, x_ref, bc_ref, slope_ref, proj_ref, edge_ref, taps_ref,
    bias_ref, alog_ref, skip_ref, spread_ref,
    y_ref, dy_ref, state_ref, start_ref, in_ref, leave_ref, out_src, gate_src,
    dproj_ref, tail_ref, early_ref, grads_ref, sums_ref, out_red, gate_red,
    carry, g, ext,
    half_in, full_in, full_out, far_out, far_in,
    s0, s1, s2, s3, s4, s5, s6, s7, s8, s9,
):
    sems = (s0, s1, s2, s3, s4, s5, s6, s7, s8, s9)
    size, width = x_ref.shape
    states = bc_ref.shape[1] // 2
    mixed_width = width + 2 * states
    step = pl.program_id(0)
    steps = pl.num_programs(0)
    chunk = steps - 1 - step
    scatters = [
        (
            Scatter(
                spans, ranges, n, src, half_in.at[n], full_in.at[n], full_out.at[n],
                far_out.at[n], far_in.at[n], sems,
            ),
            result,
        )
        for n, (src, result) in enumerate(((out_src, out_red), (gate_src, gate_red)))
    ]
    order = list(range(spans - 1, -1, -1))

    @pl.when(step == 0)
    def _():
        greet(spans, ranges)
        for k in order:
            for scatter, result in scatters:
                scatter.start_halves(k)
        carry[...] = leave_ref[...]
        sums_ref[...] = jnp.zeros_like(sums_ref)
        grads_ref[...] = jnp.zeros_like(grads_ref)
        ext[...] = jnp.zeros_like(ext)

    for place, k in enumerate(order):
        @pl.when(step == jnp.minimum(1 + place, steps - 1))
        def _():
            for scatter, result in scatters:
                scatter.start_fulls(k)

        @pl.when(step == jnp.minimum(4 + place, steps - 1))
        def _():
            for scatter, result in scatters:
                scatter.start_far(k, result)

    spread = spread_ref[...]
    (rows, cols, same, seg_one, raw, delta, decay_rate, cum, cum_t, lead, trail, upper) = (
        chunk_terms(
            info_ref, count, chunk, size, proj_ref[:, mixed_width : mixed_width + heads],
            bias_ref, alog_ref, spread,
        )
    )
    neg = jnp.where((rows <= cols) & same, 0.0, NEG)
    x = x_ref[...].astype(F32)
    delta_wide = expand(delta, spread)
    xdt = (x * delta_wide).astype(BF)
    xdt_f = xdt.astype(F32)
    dy = dy_ref[...]
    dy_f = dy.astype(F32)
    b_rows = bc_ref[:, :states]
    c_rows = bc_ref[:, states:]
    scores = dot(b_rows, c_rows, NT)
    grad_state = carry[...]
    grad_state_b = grad_state.astype(BF)
    held = state_ref[0].astype(F32) + expand(start_ref[0], spread)[0:1, :] * in_ref[...]
    held_b = held.astype(BF)
    trail_wide = expand(trail, spread)
    lead_wide = expand(lead, spread)
    state_part = dot(b_rows, grad_state_b) * trail_wide
    g[:, :width] = state_part
    head, per = pair_width(heads, width)
    span = head * per
    lane = lax.broadcasted_iota(jnp.int32, (size, span), 1) // head
    dscore = jnp.zeros((size, size), F32)
    for group in range(heads // per):
        at = slice(group * span, (group + 1) * span)
        xg = xdt[:, at]
        dyg = dy[:, at]
        out = None
        for k in range(per):
            h = group * per + k
            decay = jnp.exp(cum_t[h : h + 1, :] - cum[:, h : h + 1] + neg)
            part = dot((decay * scores).astype(BF), dyg)
            out = part if out is None else jnp.where(lane >= k, part, out)
            own = jnp.where(lane == k, xg, jnp.zeros_like(xg))
            dscore = dscore + decay * dot(own, dyg, NT)
        g[:, at] = g[:, at] + out
    dxdt = g[:, :width]
    dscore_b = dscore.astype(BF)
    led = (dy_f * lead_wide).astype(BF)
    weighted = (xdt_f * trail_wide).astype(BF)
    g[:, width : width + states] = dot(dscore_b, c_rows) + dot(weighted, grad_state_b, NT)
    g[:, width + states :] = dot(dscore_b, b_rows, TN) + dot(led, held_b, NT)
    flows = per_head(dy_f * y_ref[...] - xdt_f * dxdt, spread)
    kept = jnp.sum(xdt_f * state_part, axis=0, keepdims=True) + lead_wide[
        size - 1 :, :
    ] * jnp.sum(held * grad_state, axis=0, keepdims=True)
    at_end = per_head(jnp.broadcast_to(kept, (8, width)), spread)[0:1, :]
    drate = dot(upper, flows, precision=HIGH) + at_end
    ddelta = per_head(x * dxdt, spread) + drate * decay_rate
    draw = ddelta * jax.nn.sigmoid(raw)
    skip_sum = per_head(
        jnp.broadcast_to(jnp.sum(dy_f * x, axis=0, keepdims=True), (8, width)), spread
    )[0:1, :]
    sums_ref[0:1, :] += jnp.sum(draw, axis=0, keepdims=True)
    sums_ref[1:2, :] += jnp.sum(drate * delta, axis=0, keepdims=True) * decay_rate
    sums_ref[2:3, :] += skip_sum
    skip_wide = expand(jnp.broadcast_to(skip_ref[...], (8, heads)), spread)[0:1, :]
    g[:, :width] = dxdt * delta_wide + skip_wide * dy_f
    carry[...] = lead_wide[size - 1 :, :] * grad_state + dot(c_rows, led, TN)

    ext[8 + size :, :] = ext[8:16, :]
    ext[8 : 8 + size, :] = g[...] * slope_ref[...].astype(F32)
    first = info_ref[0] + chunk * size

    def linked(shape, base, k):
        later = base + k + lax.broadcasted_iota(jnp.int32, shape, 0)
        begin = jnp.zeros_like(later)
        for n in range(1, count):
            begin = jnp.where(later >= info_ref[n], info_ref[n], begin)
        return later - begin >= k

    values = proj_ref[:, :mixed_width].astype(F32)
    back = None
    for k in range(taps):
        moved = ext[8 + k : 8 + k + size, :]
        if k:
            moved = jnp.where(linked((size, mixed_width), first, k), moved, 0.0)
        at = taps - 1 - k
        grads_ref[at : at + 1, :] += jnp.sum(moved * values, axis=0, keepdims=True)
        if not k:
            grads_ref[taps : taps + 1, :] += jnp.sum(moved, axis=0, keepdims=True)
        term = moved * taps_ref[at : at + 1, :]
        back = term if back is None else back + term
    dproj_ref[:, :mixed_width] = back.astype(BF)
    dproj_ref[:, mixed_width:] = jnp.zeros((size, dproj_ref.shape[1] - mixed_width), BF)
    dproj_ref[:, mixed_width : mixed_width + heads] = draw.astype(BF)

    @pl.when(step == 0)
    def _():
        tail_ref[...] = back[size - 8 :, :]

    @pl.when(step == steps - 1)
    def _():
        early = jnp.zeros((8, mixed_width), F32)
        for k in range(1, taps):
            moved = jnp.where(linked((8, mixed_width), first - 8, k), ext[k : k + 8, :], 0.0)
            at = taps - 1 - k
            grads_ref[at : at + 1, :] += jnp.sum(
                moved * edge_ref[:, :mixed_width], axis=0, keepdims=True
            )
            early = early + moved * taps_ref[at : at + 1, :]
        early_ref[...] = early
        for scatter, result in scatters:
            scatter.finish(result)
        for scatter, result in scatters:
            scatter.drain()


def whole(shape):
    return pl.BlockSpec(shape, lambda i: (0,) * len(shape))


SMEM = pl.BlockSpec(memory_space=pltpu.SMEM)


def forward(info, count, hidden, gain, packed, gate, out, taps, shift, bias, alog, spread):
    length, model = hidden.shape
    heads, width = spread.shape
    states = (taps.shape[1] - width) // 2
    spans, ranges = lax.axis_size("fsdp"), lax.axis_size("context")
    chunks = length // CHUNK
    wide = packed.shape[1]
    pad = 16
    row = lambda c: pl.BlockSpec((CHUNK, c), lambda i: (i, 0))
    anywhere = pl.BlockSpec(memory_space=pl.ANY)
    gathered = lambda v: jax.ShapeDtypeStruct((spans * ranges,) + v.shape, v.dtype)
    sem = pltpu.SemaphoreType.DMA((3, spans))
    return pl.pallas_call(
        functools.partial(forward_kernel, count, heads, taps.shape[0], spans, ranges),
        grid=(chunks,),
        in_specs=[
            SMEM, whole((length, model)), whole((1, model)), whole(packed.shape),
            whole(gate.shape), whole(out.shape), whole(taps.shape), whole((1, taps.shape[1])),
            whole((1, heads)), whole((1, heads)), whole((heads, width)),
        ],
        out_specs=[
            row(model), row(wide), whole((8, wide)), row(width), row(2 * states),
            row(width + 2 * states), row(width), row(heads),
            pl.BlockSpec((1, states, width), lambda i: (i, 0, 0)), whole((states + 8, width)),
            anywhere, anywhere, anywhere,
        ],
        out_shape=[
            jax.ShapeDtypeStruct((length, model), BF),
            jax.ShapeDtypeStruct((length, wide), BF),
            jax.ShapeDtypeStruct((8, wide), F32),
            jax.ShapeDtypeStruct((length, width), BF),
            jax.ShapeDtypeStruct((length, 2 * states), BF),
            jax.ShapeDtypeStruct((length, width + 2 * states), BF),
            jax.ShapeDtypeStruct((length, width), F32),
            jax.ShapeDtypeStruct((length, heads), F32),
            jax.ShapeDtypeStruct((chunks, states, width), BF),
            jax.ShapeDtypeStruct((states + 8, width), F32),
            gathered(packed), gathered(gate), gathered(out),
        ],
        scratch_shapes=[
            pltpu.VMEM((length, model), BF),
            pltpu.VMEM((length + pad, wide), BF),
            pltpu.VMEM((spans * ranges,) + packed.shape, BF),
            pltpu.VMEM((CHUNK + pad, width + 2 * states), F32),
            pltpu.VMEM((pad, model), BF),
            pltpu.VMEM((states, width), F32),
            pltpu.VMEM((8, heads), F32),
        ] + [sem] * 10 + [pltpu.SemaphoreType.DMA((3,)), pltpu.SemaphoreType.DMA((2,))],
        compiler_params=pltpu.CompilerParams(collective_id=0, has_side_effects=True),
        name="forward",
    )(info, hidden, gain, packed, gate, out, taps, shift, bias, alog, spread)


def backward(
    info, count, x, bc, slope, proj, edge, taps, bias, alog, skip, spread, y, dy, states_at, start,
    state_in, leaving, out_term, gate_term,
):
    length, width = x.shape
    heads = bias.shape[1]
    states = bc.shape[1] // 2
    mixed_width, wide = slope.shape[1], proj.shape[1]
    spans, ranges = lax.axis_size("fsdp"), lax.axis_size("context")
    chunks = length // CHUNK
    row = lambda c: pl.BlockSpec((CHUNK, c), lambda i: (chunks - 1 - i, 0))
    rows, term_width = out_term.shape[1:]
    return pl.pallas_call(
        functools.partial(backward_kernel, count, heads, taps.shape[0], spans, ranges),
        grid=(chunks,),
        in_specs=[
            SMEM, row(width), row(2 * states), row(mixed_width), row(wide), whole((8, wide)),
            whole(taps.shape),
            whole((1, heads)), whole((1, heads)), whole((1, heads)), whole((heads, width)),
            row(width), row(width),
            pl.BlockSpec((1, states, width), lambda i: (chunks - 1 - i, 0, 0)),
            pl.BlockSpec((1, 8, heads), lambda i: (chunks - 1 - i, 0, 0)),
            whole((states, width)), whole((states, width)),
            whole(out_term.shape), whole(gate_term.shape),
        ],
        out_specs=[
            row(wide), whole((8, mixed_width)), whole((8, mixed_width)), whole((8, mixed_width)),
            whole((8, heads)), whole((rows, term_width)), whole((rows, term_width)),
        ],
        out_shape=[
            jax.ShapeDtypeStruct((length, wide), BF),
            jax.ShapeDtypeStruct((8, mixed_width), F32),
            jax.ShapeDtypeStruct((8, mixed_width), F32),
            jax.ShapeDtypeStruct((8, mixed_width), F32),
            jax.ShapeDtypeStruct((8, heads), F32),
            jax.ShapeDtypeStruct((rows, term_width), F32),
            jax.ShapeDtypeStruct((rows, term_width), F32),
        ],
        scratch_shapes=[
            pltpu.VMEM((states, width), F32),
            pltpu.VMEM((CHUNK, mixed_width), F32),
            pltpu.VMEM((CHUNK + 16, mixed_width), F32),
        ] + scatter_scratch(spans, 2, rows, term_width),
        compiler_params=pltpu.CompilerParams(collective_id=1, has_side_effects=True),
        name="backward",
    )(
        info, x, bc, slope, proj, edge, taps, bias, alog, skip, spread, y, dy, states_at, start,
        state_in, leaving, out_term, gate_term,
    )


def ring(axis, step):
    count = lax.axis_size(axis)
    return [(source, (source + step) % count) for source in range(count)]


def shifted(value, axis, steps):
    count = lax.axis_size(axis)
    initial, last = (max(0, -steps), min(count, count - steps))
    return lax.ppermute(value, axis, [(source, source + steps) for source in range(initial, last)])


def total_over(value, axis):
    if lax.axis_size(axis) == 2:
        return value.astype(F32) + lax.ppermute(value, axis, ring(axis, 1)).astype(F32)
    return jnp.sum(gather_axis(value, axis, 0).astype(F32), axis=0)


def share_over(value, axis, dim):
    count, index = (lax.axis_size(axis), lax.axis_index(axis))
    size = value.shape[dim] // count
    part = lambda at: lax.dynamic_slice_in_dim(value, at * size, size, dim)
    result = part(index).astype(F32)
    for step in range(1, count):
        sent = part((index + step) % count)
        result = result + lax.ppermute(sent, axis, ring(axis, step)).astype(F32)
    return result


def gather_axis(value, axis, dim):
    count, index = (lax.axis_size(axis), lax.axis_index(axis))
    shape = value.shape[:dim] + (count,) + value.shape[dim:]
    result = lax.dynamic_update_index_in_dim(jnp.zeros(shape, value.dtype), value, index, dim)
    for step in range(1, count):
        got = lax.ppermute(value, axis, ring(axis, step))
        result = lax.dynamic_update_index_in_dim(result, got, (index - step) % count, dim)
    return result


def columns(value, widths):
    pieces, at = ([], 0)
    for width in widths:
        pieces.append(value[..., at : at + width])
        at += width
    return pieces


def scatter_axis(values, axis, dim):
    count, index = (lax.axis_size(axis), lax.axis_index(axis))
    part = lambda at: jnp.concatenate(
        [lax.dynamic_index_in_dim(value, at, dim, False) for value in values], axis=-1
    )
    received = [
        lax.ppermute(part((index + step) % count), axis, ring(axis, step))
        for step in range(1, count)
    ]
    result = part(index).astype(F32)
    for got in received:
        result = result + got.astype(F32)
    return result


def scatter_first(values):
    fsdp, context = (lax.axis_size("fsdp"), lax.axis_size("context"))
    shaped = [v.astype(BF).reshape(fsdp, context, -1, v.shape[-1]) for v in values]
    return scatter_axis(shaped, "context", 1).astype(BF)


def scatter_second(half, values):
    return columns(scatter_axis([half], "fsdp", 0), [v.shape[-1] for v in values])


def chain(state, decay_rows, direction):
    states = state.shape[0]
    packed = jnp.concatenate([state, decay_rows], axis=0).astype(BF)
    total = jnp.zeros_like(state)
    factor = jnp.ones((1, state.shape[1]), F32)
    for step in range(1, lax.axis_size("context")):
        got = shifted(packed, "context", direction * step).astype(F32)
        total = total + factor * got[:states]
        factor = factor * got[states : states + 1]
    return total


def body(
    hidden, d_mixed, seq_lengths, norm_gain, w_gate, w_x, w_bc, w_dt, conv_x, conv_x_bias,
    conv_bc, conv_bc_bias, dt_bias, a_log, d_skip, gate_gain, w_out,
):
    row_count, model_width = hidden.shape
    lanes = lax.axis_size("tensor")
    lane = lax.axis_index("tensor")
    share_width = model_width // lanes
    share_start = lane * share_width
    inner_local = conv_x.shape[1]
    inner_width = inner_local * lanes
    heads = dt_bias.shape[0]
    bc_width = conv_bc.shape[1]
    states = bc_width // 2
    lengths = seq_lengths[0]
    count = lengths.shape[0]
    first_row = lax.axis_index("context") * row_count
    starts = (jnp.cumsum(lengths) - lengths).astype(jnp.int32)
    info = jnp.concatenate([first_row.astype(jnp.int32)[None], starts[1:]])
    spread = (
        lax.broadcasted_iota(jnp.int32, (heads, inner_local), 1) // (inner_local // heads)
        == lax.broadcasted_iota(jnp.int32, (heads, inner_local), 0)
    ).astype(BF)

    widened = hidden.astype(F32)
    row_scale = lax.rsqrt(jnp.mean(widened * widened, axis=1, keepdims=True) + EPSILON)
    mixed_width = inner_local + bc_width
    spare = -(-heads // 128) * 128 - heads
    packed = jnp.concatenate(
        [w_x, w_bc, w_dt, jnp.zeros((w_x.shape[0], spare), w_x.dtype)], axis=1
    )
    bias_row, alog_row, skip_row = (dt_bias[None, :], a_log[None, :], d_skip[None, :])
    taps_all = jnp.concatenate([conv_x, conv_bc], axis=1)
    (
        normed, proj, edge, x_act, bc_act, slope, y_local, full, states_at, final,
        packed_weight, gate_weight, out_weight,
    ) = forward(
        info, count, hidden, norm_gain[None, :], packed, w_gate, w_out.T,
        taps_all,
        jnp.concatenate([conv_x_bias, conv_bc_bias])[None, :],
        bias_row, alog_row, spread,
    )
    packed_weight = packed_weight.reshape(model_width, -1)
    gate_weight = gate_weight.reshape(model_width, -1)
    out_weight = out_weight.reshape(model_width, -1)
    z_proj = dot(normed, gate_weight).astype(BF)
    decay_rows = final[states:]
    state_in = chain(final[:states], decay_rows, 1)
    c_rows = bc_act[:, states:]
    full_wide = expand(full, spread)
    y = y_local + dot(c_rows, state_in.astype(BF)) * full_wide
    skip_wide = jnp.repeat(d_skip, inner_local // heads)[None, :]
    y_full = y + skip_wide * x_act.astype(F32)
    z = z_proj.astype(F32)
    sig = jax.nn.sigmoid(z)
    gate = z * sig
    gated = y_full * gate
    grad_norm_out = dot(d_mixed, out_weight)
    scaled = grad_norm_out * gate_gain[None, :]
    both = total_over(
        jnp.stack([jnp.sum(gated * gated, axis=1), jnp.sum(scaled * gated, axis=1)]), "tensor"
    )
    gate_scale = lax.rsqrt(both[0][:, None] / inner_width + EPSILON)
    unit = gated * gate_scale
    normed_out = (unit * gate_gain[None, :]).astype(BF)
    grad_gated = gate_scale * scaled - gated * gate_scale**3 * (both[1][:, None] / inner_width)
    dy = (grad_gated * gate).astype(BF)
    grad_zb = (grad_gated * y_full * sig * (1.0 + z * (1.0 - sig))).astype(BF)
    gain_term = jnp.sum(grad_norm_out * unit, axis=0)
    grad_in = dot(c_rows, (dy.astype(F32) * full_wide).astype(BF), TN)
    leaving = chain(grad_in, decay_rows, -1)
    out_partial = dot(normed_out, out_weight, NT).astype(BF)
    out_term = dot(d_mixed, normed_out, TN).astype(BF)
    gate_term = dot(normed, grad_zb, TN).astype(BF)
    leaving, out_partial, out_term, gate_term = lax.optimization_barrier(
        (leaving, out_partial, out_term, gate_term)
    )
    mixed_share = share_over(out_partial, "tensor", 1)
    hidden_share = lax.dynamic_slice_in_dim(widened, share_start, share_width, 1)
    mixed = (hidden_share + mixed_share).astype(BF)
    by_owner = lambda v: v.reshape(-1, w_gate.shape[0], v.shape[1])
    starting = jnp.concatenate([jnp.ones((1, heads), F32), full[CHUNK - 1 :: CHUNK][:-1]], axis=0)
    starting = jnp.broadcast_to(starting[:, None, :], (starting.shape[0], 8, heads))
    dproj, tail, early, conv_grads, head_sums, grad_w_out, grad_w_gate = backward(
        info, count, x_act, bc_act, slope, proj, edge, taps_all, bias_row, alog_row, skip_row,
        spread, y, dy, states_at, starting, state_in, leaving,
        by_owner(out_term), by_owner(gate_term),
    )
    grad_w_out = grad_w_out.T
    early = shifted(early, "context", -1)
    dproj = lax.dynamic_update_slice(dproj, (tail + early).astype(BF), (row_count - 8, 0))
    late = [dot(normed, dproj, TN)]
    (grad_packed,) = scatter_second(scatter_first(late), late)
    grad_normed = dot(grad_zb, gate_weight, NT) + dot(dproj, packed_weight, NT)
    grad_share = share_over(grad_normed.astype(BF), "tensor", 1)
    gain_share = lax.dynamic_slice_in_dim(norm_gain, share_start, share_width, 0)
    norm_term = jnp.sum(grad_share * hidden_share * row_scale, axis=0)
    gained = grad_share * gain_share[None, :]
    dot_rows = total_over(jnp.sum(gained * hidden_share, axis=1), "tensor")
    dot_rows = dot_rows[:, None] / model_width
    dmix_share = lax.dynamic_slice_in_dim(d_mixed, share_start, share_width, 1)
    grad_hidden = (
        dmix_share.astype(F32) + row_scale * gained - hidden_share * row_scale**3 * dot_rows
    )
    taps = conv_x.shape[0]
    pieces = [
        conv_grads[: taps + 1], head_sums[:3], gain_term, norm_term,
    ]
    flat = jnp.concatenate([p.reshape(-1) for p in pieces])
    padded = -(-flat.shape[0] // 1024) * 1024
    flat = jnp.concatenate([flat, jnp.zeros((padded - flat.shape[0],), F32)]).reshape(-1, 128)
    flat = total_over(total_over(flat, "context"), "fsdp").reshape(-1)
    summed, at = ([], 0)
    for p in pieces:
        size = p.size
        summed.append(flat[at : at + size].reshape(p.shape))
        at += size
    sconv, sh, sgain, snorm = summed
    sx = sconv[:, :inner_local]
    shared = jnp.concatenate(
        [sconv[:, inner_local:], grad_packed[:, inner_local:mixed_width]], axis=0
    )
    shared = total_over(shared, "tensor")
    sbc, grad_bc = shared[: taps + 1], shared[taps + 1 :]
    grad_w_x = grad_packed[:, :inner_local]
    grad_w_dt = grad_packed[:, mixed_width : mixed_width + heads]
    return (
        mixed, grad_hidden, snorm, grad_w_gate, grad_w_x, grad_bc, grad_w_dt, sx[:taps], sx[taps], sbc[:taps], sbc[taps],
        sh[0], sh[1], sh[2], sgain, grad_w_out,
    )


def solution(mesh):
    return jax.shard_map(
        body,
        mesh=mesh,
        in_specs=(
            P(("fsdp", "context"), None),
            P(("fsdp", "context"), None),
            P("fsdp", None),
            P(),
            P(("fsdp", "context"), "tensor"),
            P(("fsdp", "context"), "tensor"),
            P(("fsdp", "context"), None),
            P(("fsdp", "context"), "tensor"),
            P(None, "tensor"),
            P("tensor"),
            P(),
            P(),
            P("tensor"),
            P("tensor"),
            P("tensor"),
            P("tensor"),
            P("tensor", ("fsdp", "context")),
        ),
        out_specs=(
            P(("fsdp", "context"), "tensor"),
            P(("fsdp", "context"), "tensor"),
            P("tensor"),
            P(("fsdp", "context"), "tensor"),
            P(("fsdp", "context"), "tensor"),
            P(("fsdp", "context"), None),
            P(("fsdp", "context"), "tensor"),
            P(None, "tensor"),
            P("tensor"),
            P(),
            P(),
            P("tensor"),
            P("tensor"),
            P("tensor"),
            P("tensor"),
            P("tensor", ("fsdp", "context")),
        ),
        check_vma=False,
    )
```

```python
import functools
import jax
import jax.numpy as jnp
from jax import lax
from jax.experimental import pallas as pl
from jax.experimental.pallas import tpu as pltpu
from jax.sharding import PartitionSpec as P

EPSILON = 1e-05
HIGH = lax.Precision.HIGHEST
BF = jnp.bfloat16
F32 = jnp.float32
CHUNK = 128
NEG = -1e30
MESH = pl.DeviceIdType.MESH
NT = (((1,), (1,)), ((), ()))
TN = (((0,), (0,)), ((), ()))


def dot(a, b, dims=(((1,), (0,)), ((), ())), precision=None):
    return lax.dot_general(a, b, dims, precision=precision, preferred_element_type=F32)


def split2(value):
    high = value.astype(BF)
    return high, (value - high.astype(F32)).astype(BF)


def expand(value, spread):
    high, low = split2(value)
    return dot(high, spread) + dot(low, spread)


def per_head(value, spread):
    high, low = split2(value)
    return dot(high, spread, NT) + dot(low, spread, NT)


def seg_at(info_ref, count, positions):
    found = jnp.where(positions < 0, -1, 0)
    for k in range(1, count):
        found = found + jnp.where(positions >= info_ref[k], 1, 0)
    return found


def softplus(v):
    return jnp.maximum(v, 0.0) + jnp.log1p(jnp.exp(-jnp.abs(v)))


def chunk_terms(info_ref, count, chunk, size, dt_ref, bias_ref, alog_ref, spread):
    first = info_ref[0] + chunk * size
    rows = lax.broadcasted_iota(jnp.int32, (size, size), 0)
    cols = lax.broadcasted_iota(jnp.int32, (size, size), 1)
    seg_row = seg_at(info_ref, count, first + rows)
    seg_col = seg_at(info_ref, count, first + cols)
    seg_one = seg_at(info_ref, count, first + lax.broadcasted_iota(jnp.int32, (size, 1), 0))
    seg_prev = seg_at(info_ref, count, first - 1)
    seg_last = seg_at(info_ref, count, first + size - 1)
    raw = dt_ref.astype(F32) + bias_ref[...]
    delta = softplus(raw)
    decay_rate = -jnp.exp(alog_ref[...])
    rates = delta * decay_rate
    lower = jnp.where(rows >= cols, 1.0, 0.0)
    cum = dot(lower, rates, precision=HIGH)
    upper = jnp.where(rows <= cols, 1.0, 0.0)
    cum_t = dot(rates, upper, TN, precision=HIGH)
    lead = jnp.where(seg_one == seg_prev, jnp.exp(cum), 0.0)
    trail = jnp.where(seg_one == seg_last, jnp.exp(cum[size - 1 :, :] - cum), 0.0)
    same = seg_row == seg_col
    return (rows, cols, same, seg_one, raw, delta, decay_rate, cum, cum_t, lead, trail, upper)


def pair_width(heads, width):
    head = width // heads
    per = max(1, 128 // head)
    while heads % per:
        per -= 1
    return head, per


def flip(index, mask):
    out = index
    bit = 1
    while bit <= mask:
        if mask & bit:
            out = out + bit - 2 * bit * lax.rem(lax.div(index, bit), 2)
        bit *= 2
    return out


def push(src, dst, send, recv, f, c):
    return pltpu.make_async_remote_copy(
        src_ref=src, dst_ref=dst, send_sem=send, recv_sem=recv,
        device_id={"fsdp": f, "context": c}, device_id_type=MESH,
    )


class Gather:
    def __init__(self, spans, ranges, shard, full, item, sems):
        self.f, self.c = lax.axis_index("fsdp"), lax.axis_index("context")
        self.spans, self.ranges, self.shard, self.full, self.item = spans, ranges, shard, full, item
        self.sems = sems
        self.half = shard.shape[0] // 2

    def sem(self, kind, k):
        return self.sems[kind].at[self.item, k]

    def block(self, k, flip_c):
        return self.full.at[flip(self.f, k) * self.ranges + flip(self.c, flip_c)]

    def column(self, k):
        return push(
            self.shard, self.full.at[self.f * self.ranges + self.c],
            self.sem(0, k), self.sem(1, k), flip(self.f, k), self.c,
        )

    def arrived(self, k):
        push(
            self.shard, self.block(k, 0), self.sem(0, k), self.sem(1, k), flip(self.f, k), self.c
        ).wait_recv()

    def side(self, k, way):
        source = self.block(k, 0) if k else self.shard
        return push(
            source, self.block(k, 0), self.sem(2 * way, k), self.sem(2 * way + 1, k),
            self.f, flip(self.c, way),
        )

    def side_arrived(self, k, way):
        block = self.block(k, way)
        push(
            block, block, self.sem(2 * way, k), self.sem(2 * way + 1, k), self.f, flip(self.c, way)
        ).wait_recv()

    def relay(self, k, way):
        other = 3 - way
        part = pl.ds((way - 1) * self.half, self.half)
        block = self.block(k, other).at[part]
        return push(
            block, block, self.sem(4 + 2 * way, k), self.sem(5 + 2 * way, k),
            self.f, flip(self.c, way),
        )

    def relay_arrived(self, k, way):
        part = pl.ds((way - 1) * self.half, self.half)
        block = self.block(k, 3).at[part]
        push(
            block, block, self.sem(4 + 2 * way, k), self.sem(5 + 2 * way, k),
            self.f, flip(self.c, way),
        ).wait_recv()

    def start_columns(self):
        for k in range(1, self.spans):
            self.column(k).start()

    def start_sides(self, k):
        if k:
            self.arrived(k)
        for way in (1, 2):
            self.side(k, way).start()

    def start_relays(self, k):
        for way in (2, 1):
            self.side_arrived(k, 3 - way)
            self.relay(k, way).start()

    def finish(self):
        for k in range(self.spans):
            for way in (1, 2):
                self.relay_arrived(k, way)

    def drain(self):
        for k in range(self.spans):
            if k:
                self.column(k).wait_send()
            for way in (1, 2):
                self.side(k, way).wait_send()
                self.relay(k, way).wait_send()


def forward_kernel(
    count, heads, taps, spans, ranges,
    info_ref, hidden_ref, gain_ref, packed_ref, gate_ref, out_ref, taps_ref, shift_ref,
    bias_ref, alog_ref, spread_ref,
    normed_ref, proj_ref, edge_ref, xact_ref, bc_ref, slope_ref,
    y_ref, full_ref, state_ref, final_ref, packed_all, gate_all, out_all,
    normed, proj, weights, ext, before, carry, total,
    s0, s1, s2, s3, s4, s5, s6, s7, s8, s9, local, edge_sems,
):
    sems = (s0, s1, s2, s3, s4, s5, s6, s7, s8, s9)
    size, width = xact_ref.shape
    states = bc_ref.shape[1] // 2
    step = pl.program_id(0)
    steps = pl.num_programs(0)
    length = hidden_ref.shape[0]
    pad = before.shape[0]
    mixed_width = width + 2 * states
    f, c = lax.axis_index("fsdp"), lax.axis_index("context")
    first = Gather(spans, ranges, packed_ref, weights, 0, sems)
    later = [
        Gather(spans, ranges, gate_ref, gate_all, 1, sems),
        Gather(spans, ranges, out_ref, out_all, 2, sems),
    ]
    own = f * ranges + c
    own_copies = [
        pltpu.make_async_copy(gate_ref, gate_all.at[own], local.at[0]),
        pltpu.make_async_copy(out_ref, out_all.at[own], local.at[1]),
    ]
    keep = pltpu.make_async_copy(weights, packed_all, local.at[2])
    edge_to = push(
        hidden_ref.at[pl.ds(length - pad, pad)], before, edge_sems.at[0], edge_sems.at[1],
        f, lax.rem(c + 1, ranges),
    )
    gain = gain_ref[...]

    def norm(rows):
        wide = rows.astype(F32)
        scale = lax.rsqrt(jnp.mean(wide * wide, axis=1, keepdims=True) + EPSILON)
        return (wide * scale * gain).astype(BF)

    @pl.when(step == 0)
    def _():
        greet(spans, ranges)
        first.start_sides(0)
        first.start_columns()
        edge_to.start()
        for copy in own_copies:
            copy.start()
        weights[own] = packed_ref[...]
        carry[...] = jnp.zeros_like(carry)
        total[...] = jnp.zeros_like(total)

        @pl.loop(0, steps)
        def _(i):
            at = pl.ds(pl.multiple_of(i * size, size), size)
            normed[at, :] = norm(hidden_ref[at, :])

        for k in range(1, spans):
            first.start_sides(k)
            first.start_relays(k - 1)
        for gather in later:
            gather.start_columns()
        first.start_relays(spans - 1)
        for gather in later:
            gather.start_sides(0)
        edge_to.wait()
        first.finish()
        keep.start()

        @pl.loop(0, length // (2 * size))
        def _(i):
            at = pl.ds(pl.multiple_of(i * 2 * size, 2 * size), 2 * size)
            to = pl.ds(pl.multiple_of(i * 2 * size + pad, pad), 2 * size)
            proj[to, :] = dot(
                normed[at, :], weights[...].reshape(-1, weights.shape[2])
            ).astype(BF)

        head_rows = norm(before[...])
        head_rows = jnp.where(c == 0, jnp.zeros_like(head_rows), head_rows)
        proj[0:pad, :] = dot(head_rows, weights[...].reshape(-1, weights.shape[2])).astype(BF)
        edge_ref[...] = proj[0:pad, :].astype(F32)[pad - 8 :, :]

    for k in range(1, spans):
        @pl.when(step == (k * (length // size)) // spans)
        def _():
            for gather in later:
                gather.start_sides(k)
            for gather in later:
                gather.start_relays(k - 1)

    rows_at = pl.ds(pl.multiple_of(step * size, size), size)
    ext_at = pl.ds(pl.multiple_of(step * size, pad), size + pad)
    normed_ref[...] = normed[rows_at, :]
    proj_ref[...] = proj[pl.ds(pl.multiple_of(step * size + pad, pad), size), :]
    ext[...] = proj[ext_at, :mixed_width].astype(F32)
    position = info_ref[0] + step * size + lax.broadcasted_iota(jnp.int32, (size, mixed_width), 0)
    begin = jnp.zeros_like(position)
    for k in range(1, count):
        begin = jnp.where(position >= info_ref[k], info_ref[k], begin)
    since = position - begin
    pre = ext[pad : pad + size, :] * taps_ref[taps - 1 : taps, :] + shift_ref[...]
    for k in range(1, taps):
        moved = jnp.where(since >= k, ext[pad - k : pad - k + size, :], 0.0)
        pre = pre + moved * taps_ref[taps - 1 - k : taps - k, :]
    sig = jax.nn.sigmoid(pre)
    act = (pre * sig).astype(BF)
    slope_ref[...] = (sig * (1.0 + pre * (1.0 - sig))).astype(BF)
    xact_ref[...] = act[:, :width]
    bc_ref[...] = act[:, width:]

    spread = spread_ref[...]
    (rows, cols, same, seg_one, raw, delta, decay_rate, cum, cum_t, lead, trail, upper) = (
        chunk_terms(
            info_ref, count, step, size,
            proj_ref[:, mixed_width : mixed_width + heads], bias_ref, alog_ref, spread,
        )
    )
    neg = jnp.where((rows >= cols) & same, 0.0, NEG)
    seg_before = seg_at(info_ref, count, info_ref[0] - 1)
    full_ref[...] = jnp.where(seg_one == seg_before, jnp.exp(cum + total[0:1, :]), 0.0)
    total[0:1, :] = total[0:1, :] + cum[size - 1 :, :]
    x = xact_ref[...].astype(F32)
    xdt = (x * expand(delta, spread)).astype(BF)
    b_rows = bc_ref[:, :states]
    c_rows = bc_ref[:, states:]
    scores = dot(c_rows, b_rows, NT)
    held = carry[...]
    held_b = held.astype(BF)
    state_ref[0] = held_b
    lead_wide = expand(lead, spread)
    y_ref[...] = dot(c_rows, held_b) * lead_wide
    head, per = pair_width(heads, width)
    span = head * per
    lane = lax.broadcasted_iota(jnp.int32, (size, span), 1) // head
    for group in range(heads // per):
        at = slice(group * span, (group + 1) * span)
        xg = xdt[:, at]
        out = None
        for k in range(per):
            h = group * per + k
            decay = jnp.exp(cum[:, h : h + 1] - cum_t[h : h + 1, :] + neg)
            part = dot((decay * scores).astype(BF), xg)
            out = part if out is None else jnp.where(lane >= k, part, out)
        y_ref[:, at] = y_ref[:, at] + out
    weighted = (xdt.astype(F32) * expand(trail, spread)).astype(BF)
    carry[...] = lead_wide[size - 1 :, :] * held + dot(b_rows, weighted, TN)

    @pl.when(step == steps - 1)
    def _():
        final_ref[:states, :] = carry[...]
        final_ref[states:, :] = expand(
            jnp.broadcast_to(full_ref[size - 1 :, :], (8, heads)), spread
        )
        for gather in later:
            gather.start_relays(spans - 1)
        keep.wait()
        for copy in own_copies:
            copy.wait()
        for gather in later:
            gather.finish()
        for gather in [first] + later:
            gather.drain()


class Scatter:
    def __init__(self, spans, ranges, item, src, half_in, full_in, full_out, far_out, far_in, sems):
        self.f, self.c = lax.axis_index("fsdp"), lax.axis_index("context")
        self.spans, self.ranges, self.item, self.src = spans, ranges, item, src
        self.half_in, self.full_in, self.full_out = half_in, full_in, full_out
        self.far_out, self.far_in, self.sems = far_out, far_in, sems
        self.half = src.shape[1] // 2

    def sem(self, kind, k):
        return self.sems[kind].at[self.item, k]

    def at(self, k, flip_c):
        return flip(self.f, k) * self.ranges + flip(self.c, flip_c)

    def part(self, way):
        return pl.ds((way - 1) * self.half, self.half)

    def half_copy(self, k, way):
        return push(
            self.src.at[self.at(k, 3), self.part(way)], self.half_in.at[way - 1, k],
            self.sem(2 * way - 2, k), self.sem(2 * way - 1, k), self.f, flip(self.c, way),
        )

    def full_copy(self, k, way):
        return push(
            self.full_out.at[way - 1, k], self.full_in.at[way - 1, k],
            self.sem(2 * way + 2, k), self.sem(2 * way + 3, k), self.f, flip(self.c, way),
        )

    def far_copy(self, k):
        return push(
            self.far_out.at[k], self.far_in.at[k], self.sem(8, k), self.sem(9, k),
            flip(self.f, k), self.c,
        )

    def start_halves(self, k):
        for way in (1, 2):
            self.half_copy(k, way).start()

    def start_fulls(self, k):
        for way in (1, 2):
            other = 3 - way
            self.half_copy(k, way).wait_recv()
            index, part, rest = self.at(k, other), self.part(way), self.part(other)
            self.full_out[other - 1, k, part, :] = (
                self.src[index, part, :].astype(F32) + self.half_in[way - 1, k].astype(F32)
            ).astype(BF)
            self.full_out[other - 1, k, rest, :] = self.src[index, rest, :]
            self.full_copy(k, other).start()

    def start_far(self, k, result):
        for way in (1, 2):
            self.full_copy(k, way).wait_recv()
        total = self.src[self.at(k, 0)].astype(F32) + (
            self.full_in[0, k].astype(F32) + self.full_in[1, k].astype(F32)
        )
        if k:
            self.far_out[k] = total.astype(BF)
            self.far_copy(k).start()
        else:
            result[...] = total

    def finish(self, result):
        for k in range(1, self.spans):
            self.far_copy(k).wait_recv()
            result[...] += self.far_in[k].astype(F32)

    def drain(self):
        for k in range(self.spans):
            for way in (1, 2):
                self.half_copy(k, way).wait_send()
                self.full_copy(k, way).wait_send()
            if k:
                self.far_copy(k).wait_send()


def scatter_scratch(spans, items, rows, width):
    return [
        pltpu.VMEM((items, 2, spans, rows // 2, width), BF),
        pltpu.VMEM((items, 2, spans, rows, width), BF),
        pltpu.VMEM((items, 2, spans, rows, width), BF),
        pltpu.VMEM((items, spans, rows, width), BF),
        pltpu.VMEM((items, spans, rows, width), BF),
    ] + [pltpu.SemaphoreType.DMA((items, spans))] * 10


def greet(spans, ranges, others=0):
    f, c = lax.axis_index("fsdp"), lax.axis_index("context")
    barrier = pltpu.get_barrier_semaphore()
    for k in range(1, spans):
        pl.semaphore_signal(
            barrier, inc=1, device_id={"fsdp": flip(f, k), "context": c}, device_id_type=MESH
        )
    for k in range(1, ranges):
        pl.semaphore_signal(
            barrier, inc=1, device_id={"fsdp": f, "context": lax.rem(c + k, ranges)},
            device_id_type=MESH,
        )
    pl.semaphore_wait(barrier, spans + ranges - 2 + others)


def backward_kernel(
    count, heads, taps, spans, ranges,
    info_ref, x_ref, bc_ref, slope_ref, proj_ref, edge_ref, taps_ref,
    bias_ref, alog_ref, skip_ref, spread_ref,
    y_ref, dy_ref, state_ref, start_ref, in_ref, leave_ref, out_src, gate_src,
    dproj_ref, tail_ref, early_ref, grads_ref, sums_ref, out_red, gate_red,
    carry, g, ext,
    half_in, full_in, full_out, far_out, far_in,
    s0, s1, s2, s3, s4, s5, s6, s7, s8, s9,
):
    sems = (s0, s1, s2, s3, s4, s5, s6, s7, s8, s9)
    size, width = x_ref.shape
    states = bc_ref.shape[1] // 2
    mixed_width = width + 2 * states
    step = pl.program_id(0)
    steps = pl.num_programs(0)
    chunk = steps - 1 - step
    scatters = [
        (
            Scatter(
                spans, ranges, n, src, half_in.at[n], full_in.at[n], full_out.at[n],
                far_out.at[n], far_in.at[n], sems,
            ),
            result,
        )
        for n, (src, result) in enumerate(((out_src, out_red), (gate_src, gate_red)))
    ]
    order = list(range(spans - 1, -1, -1))

    @pl.when(step == 0)
    def _():
        greet(spans, ranges)
        for k in order:
            for scatter, result in scatters:
                scatter.start_halves(k)
        carry[...] = leave_ref[...]
        sums_ref[...] = jnp.zeros_like(sums_ref)
        grads_ref[...] = jnp.zeros_like(grads_ref)
        ext[...] = jnp.zeros_like(ext)

    for place, k in enumerate(order):
        @pl.when(step == jnp.minimum(1 + place, steps - 1))
        def _():
            for scatter, result in scatters:
                scatter.start_fulls(k)

        @pl.when(step == jnp.minimum(4 + place, steps - 1))
        def _():
            for scatter, result in scatters:
                scatter.start_far(k, result)

    spread = spread_ref[...]
    (rows, cols, same, seg_one, raw, delta, decay_rate, cum, cum_t, lead, trail, upper) = (
        chunk_terms(
            info_ref, count, chunk, size, proj_ref[:, mixed_width : mixed_width + heads],
            bias_ref, alog_ref, spread,
        )
    )
    neg = jnp.where((rows <= cols) & same, 0.0, NEG)
    x = x_ref[...].astype(F32)
    delta_wide = expand(delta, spread)
    xdt = (x * delta_wide).astype(BF)
    xdt_f = xdt.astype(F32)
    dy = dy_ref[...]
    dy_f = dy.astype(F32)
    b_rows = bc_ref[:, :states]
    c_rows = bc_ref[:, states:]
    scores = dot(b_rows, c_rows, NT)
    grad_state = carry[...]
    grad_state_b = grad_state.astype(BF)
    held = state_ref[0].astype(F32) + expand(start_ref[0], spread)[0:1, :] * in_ref[...]
    held_b = held.astype(BF)
    trail_wide = expand(trail, spread)
    lead_wide = expand(lead, spread)
    state_part = dot(b_rows, grad_state_b) * trail_wide
    g[:, :width] = state_part
    head, per = pair_width(heads, width)
    span = head * per
    lane = lax.broadcasted_iota(jnp.int32, (size, span), 1) // head
    dscore = jnp.zeros((size, size), F32)
    for group in range(heads // per):
        at = slice(group * span, (group + 1) * span)
        xg = xdt[:, at]
        dyg = dy[:, at]
        out = None
        for k in range(per):
            h = group * per + k
            decay = jnp.exp(cum_t[h : h + 1, :] - cum[:, h : h + 1] + neg)
            part = dot((decay * scores).astype(BF), dyg)
            out = part if out is None else jnp.where(lane >= k, part, out)
            own = jnp.where(lane == k, xg, jnp.zeros_like(xg))
            dscore = dscore + decay * dot(own, dyg, NT)
        g[:, at] = g[:, at] + out
    dxdt = g[:, :width]
    dscore_b = dscore.astype(BF)
    led = (dy_f * lead_wide).astype(BF)
    weighted = (xdt_f * trail_wide).astype(BF)
    g[:, width : width + states] = dot(dscore_b, c_rows) + dot(weighted, grad_state_b, NT)
    g[:, width + states :] = dot(dscore_b, b_rows, TN) + dot(led, held_b, NT)
    flows = per_head(dy_f * y_ref[...] - xdt_f * dxdt, spread)
    kept = jnp.sum(xdt_f * state_part, axis=0, keepdims=True) + lead_wide[
        size - 1 :, :
    ] * jnp.sum(held * grad_state, axis=0, keepdims=True)
    at_end = per_head(jnp.broadcast_to(kept, (8, width)), spread)[0:1, :]
    drate = dot(upper, flows, precision=HIGH) + at_end
    ddelta = per_head(x * dxdt, spread) + drate * decay_rate
    draw = ddelta * jax.nn.sigmoid(raw)
    skip_sum = per_head(
        jnp.broadcast_to(jnp.sum(dy_f * x, axis=0, keepdims=True), (8, width)), spread
    )[0:1, :]
    sums_ref[0:1, :] += jnp.sum(draw, axis=0, keepdims=True)
    sums_ref[1:2, :] += jnp.sum(drate * delta, axis=0, keepdims=True) * decay_rate
    sums_ref[2:3, :] += skip_sum
    skip_wide = expand(jnp.broadcast_to(skip_ref[...], (8, heads)), spread)[0:1, :]
    g[:, :width] = dxdt * delta_wide + skip_wide * dy_f
    carry[...] = lead_wide[size - 1 :, :] * grad_state + dot(c_rows, led, TN)

    ext[8 + size :, :] = ext[8:16, :]
    ext[8 : 8 + size, :] = g[...] * slope_ref[...].astype(F32)
    first = info_ref[0] + chunk * size

    def linked(shape, base, k):
        later = base + k + lax.broadcasted_iota(jnp.int32, shape, 0)
        begin = jnp.zeros_like(later)
        for n in range(1, count):
            begin = jnp.where(later >= info_ref[n], info_ref[n], begin)
        return later - begin >= k

    values = proj_ref[:, :mixed_width].astype(F32)
    back = None
    for k in range(taps):
        moved = ext[8 + k : 8 + k + size, :]
        if k:
            moved = jnp.where(linked((size, mixed_width), first, k), moved, 0.0)
        at = taps - 1 - k
        grads_ref[at : at + 1, :] += jnp.sum(moved * values, axis=0, keepdims=True)
        if not k:
            grads_ref[taps : taps + 1, :] += jnp.sum(moved, axis=0, keepdims=True)
        term = moved * taps_ref[at : at + 1, :]
        back = term if back is None else back + term
    dproj_ref[:, :mixed_width] = back.astype(BF)
    dproj_ref[:, mixed_width:] = jnp.zeros((size, dproj_ref.shape[1] - mixed_width), BF)
    dproj_ref[:, mixed_width : mixed_width + heads] = draw.astype(BF)

    @pl.when(step == 0)
    def _():
        tail_ref[...] = back[size - 8 :, :]

    @pl.when(step == steps - 1)
    def _():
        early = jnp.zeros((8, mixed_width), F32)
        for k in range(1, taps):
            moved = jnp.where(linked((8, mixed_width), first - 8, k), ext[k : k + 8, :], 0.0)
            at = taps - 1 - k
            grads_ref[at : at + 1, :] += jnp.sum(
                moved * edge_ref[:, :mixed_width], axis=0, keepdims=True
            )
            early = early + moved * taps_ref[at : at + 1, :]
        early_ref[...] = early
        for scatter, result in scatters:
            scatter.finish(result)
        for scatter, result in scatters:
            scatter.drain()


def whole(shape):
    return pl.BlockSpec(shape, lambda i: (0,) * len(shape))


SMEM = pl.BlockSpec(memory_space=pltpu.SMEM)


def forward(info, count, hidden, gain, packed, gate, out, taps, shift, bias, alog, spread):
    length, model = hidden.shape
    heads, width = spread.shape
    states = (taps.shape[1] - width) // 2
    spans, ranges = lax.axis_size("fsdp"), lax.axis_size("context")
    chunks = length // CHUNK
    wide = packed.shape[1]
    pad = 16
    row = lambda c: pl.BlockSpec((CHUNK, c), lambda i: (i, 0))
    anywhere = pl.BlockSpec(memory_space=pl.ANY)
    gathered = lambda v: jax.ShapeDtypeStruct((spans * ranges,) + v.shape, v.dtype)
    sem = pltpu.SemaphoreType.DMA((3, spans))
    return pl.pallas_call(
        functools.partial(forward_kernel, count, heads, taps.shape[0], spans, ranges),
        grid=(chunks,),
        in_specs=[
            SMEM, whole((length, model)), whole((1, model)), whole(packed.shape),
            whole(gate.shape), whole(out.shape), whole(taps.shape), whole((1, taps.shape[1])),
            whole((1, heads)), whole((1, heads)), whole((heads, width)),
        ],
        out_specs=[
            row(model), row(wide), whole((8, wide)), row(width), row(2 * states),
            row(width + 2 * states), row(width), row(heads),
            pl.BlockSpec((1, states, width), lambda i: (i, 0, 0)), whole((states + 8, width)),
            anywhere, anywhere, anywhere,
        ],
        out_shape=[
            jax.ShapeDtypeStruct((length, model), BF),
            jax.ShapeDtypeStruct((length, wide), BF),
            jax.ShapeDtypeStruct((8, wide), F32),
            jax.ShapeDtypeStruct((length, width), BF),
            jax.ShapeDtypeStruct((length, 2 * states), BF),
            jax.ShapeDtypeStruct((length, width + 2 * states), BF),
            jax.ShapeDtypeStruct((length, width), F32),
            jax.ShapeDtypeStruct((length, heads), F32),
            jax.ShapeDtypeStruct((chunks, states, width), BF),
            jax.ShapeDtypeStruct((states + 8, width), F32),
            gathered(packed), gathered(gate), gathered(out),
        ],
        scratch_shapes=[
            pltpu.VMEM((length, model), BF),
            pltpu.VMEM((length + pad, wide), BF),
            pltpu.VMEM((spans * ranges,) + packed.shape, BF),
            pltpu.VMEM((CHUNK + pad, width + 2 * states), F32),
            pltpu.VMEM((pad, model), BF),
            pltpu.VMEM((states, width), F32),
            pltpu.VMEM((8, heads), F32),
        ] + [sem] * 10 + [pltpu.SemaphoreType.DMA((3,)), pltpu.SemaphoreType.DMA((2,))],
        compiler_params=pltpu.CompilerParams(collective_id=0, has_side_effects=True),
        name="forward",
    )(info, hidden, gain, packed, gate, out, taps, shift, bias, alog, spread)


def backward(
    info, count, x, bc, slope, proj, edge, taps, bias, alog, skip, spread, y, dy, states_at, start,
    state_in, leaving, out_term, gate_term,
):
    length, width = x.shape
    heads = bias.shape[1]
    states = bc.shape[1] // 2
    mixed_width, wide = slope.shape[1], proj.shape[1]
    spans, ranges = lax.axis_size("fsdp"), lax.axis_size("context")
    chunks = length // CHUNK
    row = lambda c: pl.BlockSpec((CHUNK, c), lambda i: (chunks - 1 - i, 0))
    rows, term_width = out_term.shape[1:]
    return pl.pallas_call(
        functools.partial(backward_kernel, count, heads, taps.shape[0], spans, ranges),
        grid=(chunks,),
        in_specs=[
            SMEM, row(width), row(2 * states), row(mixed_width), row(wide), whole((8, wide)),
            whole(taps.shape),
            whole((1, heads)), whole((1, heads)), whole((1, heads)), whole((heads, width)),
            row(width), row(width),
            pl.BlockSpec((1, states, width), lambda i: (chunks - 1 - i, 0, 0)),
            pl.BlockSpec((1, 8, heads), lambda i: (chunks - 1 - i, 0, 0)),
            whole((states, width)), whole((states, width)),
            whole(out_term.shape), whole(gate_term.shape),
        ],
        out_specs=[
            row(wide), whole((8, mixed_width)), whole((8, mixed_width)), whole((8, mixed_width)),
            whole((8, heads)), whole((rows, term_width)), whole((rows, term_width)),
        ],
        out_shape=[
            jax.ShapeDtypeStruct((length, wide), BF),
            jax.ShapeDtypeStruct((8, mixed_width), F32),
            jax.ShapeDtypeStruct((8, mixed_width), F32),
            jax.ShapeDtypeStruct((8, mixed_width), F32),
            jax.ShapeDtypeStruct((8, heads), F32),
            jax.ShapeDtypeStruct((rows, term_width), F32),
            jax.ShapeDtypeStruct((rows, term_width), F32),
        ],
        scratch_shapes=[
            pltpu.VMEM((states, width), F32),
            pltpu.VMEM((CHUNK, mixed_width), F32),
            pltpu.VMEM((CHUNK + 16, mixed_width), F32),
        ] + scatter_scratch(spans, 2, rows, term_width),
        compiler_params=pltpu.CompilerParams(collective_id=1, has_side_effects=True),
        name="backward",
    )(
        info, x, bc, slope, proj, edge, taps, bias, alog, skip, spread, y, dy, states_at, start,
        state_in, leaving, out_term, gate_term,
    )


class AllSum:
    def __init__(self, spans, ranges, own, near, middle, far, sems):
        self.f, self.c = lax.axis_index("fsdp"), lax.axis_index("context")
        self.spans, self.ranges, self.own = spans, ranges, own
        self.near, self.middle, self.far, self.sems = near, middle, far, sems

    def near_copy(self, j):
        return push(
            self.own, self.near.at[self.c], self.sems[0].at[j], self.sems[1].at[j],
            self.f, lax.rem(self.c + j, self.ranges),
        )

    def far_copy(self, k):
        return push(
            self.middle, self.far.at[self.f], self.sems[2].at[k], self.sems[3].at[k],
            flip(self.f, k), self.c,
        )

    def start(self):
        self.near[self.c] = self.own[...]
        for j in range(1, self.ranges):
            self.near_copy(j).start()

    def turn(self):
        for j in range(1, self.ranges):
            source = lax.rem(self.c + self.ranges - j, self.ranges)
            push(
                self.own, self.near.at[source], self.sems[0].at[j], self.sems[1].at[j],
                self.f, source,
            ).wait_recv()
        total = self.near[0]
        for j in range(1, self.ranges):
            total = total + self.near[j]
        self.middle[...] = total
        self.far[self.f] = total
        for k in range(1, self.spans):
            self.far_copy(k).start()

    def result(self):
        for k in range(1, self.spans):
            source = flip(self.f, k)
            push(
                self.middle, self.far.at[source], self.sems[2].at[k], self.sems[3].at[k],
                source, self.c,
            ).wait_recv()
        total = self.far[0]
        for k in range(1, self.spans):
            total = total + self.far[k]
        return total

    def drain(self):
        for j in range(1, self.ranges):
            self.near_copy(j).wait_send()
        for k in range(1, self.spans):
            self.far_copy(k).wait_send()


def finish_kernel(
    spans, ranges, lanes, width, mixed_width, blocks,
    gain_ref, tail_ref, early_ref, small_ref,
    dproj_any, normed_any, zb_any, gate_any, packed_any, hidden_any, dmix_any,
    grad_ref, packed_grad, small_out, norm_out,
    dproj, normed, zb, gate, packed, hidden, dmix,
    src, part, inbox, early_in, last, norm_own,
    near, middle, far, norm_near, norm_middle, norm_far, shared, shared_in,
    half_in, full_in, full_out, far_out, far_in,
    s0, s1, s2, s3, s4, s5, s6, s7, s8, s9,
    load_sems, early_sems, box_send, box_recv, shared_send, shared_recv,
    a0, a1, a2, a3, n0, n1, n2, n3,
):
    f, c = lax.axis_index("fsdp"), lax.axis_index("context")
    lane = lax.axis_index("tensor")
    length, model = hidden.shape
    share = grad_ref.shape[1]
    rows = length // blocks
    sems = (s0, s1, s2, s3, s4, s5, s6, s7, s8, s9)
    pairs = (
        (dproj_any, dproj), (normed_any, normed), (zb_any, zb), (gate_any, gate),
        (packed_any, packed), (hidden_any, hidden), (dmix_any, dmix),
    )
    loads = [pltpu.make_async_copy(a, b, load_sems.at[n]) for n, (a, b) in enumerate(pairs)]
    scatter = Scatter(
        spans, ranges, 0, src, half_in.at[0], full_in.at[0], full_out.at[0], far_out.at[0],
        far_in.at[0], sems,
    )
    small = AllSum(spans, ranges, small_ref, near, middle, far, (a0, a1, a2, a3))
    norm = AllSum(
        spans, ranges, norm_own, norm_near, norm_middle, norm_far, (n0, n1, n2, n3)
    )
    order = list(range(spans - 1, -1, -1))
    early = push(
        early_ref, early_in, early_sems.at[0], early_sems.at[1],
        f, lax.rem(c + ranges - 1, ranges),
    )

    def across(source, target, send, recv, j):
        return pltpu.make_async_remote_copy(
            src_ref=source, dst_ref=target, send_sem=send, recv_sem=recv,
            device_id={"tensor": lax.rem(lane + j, lanes)}, device_id_type=MESH,
        )

    def box(r, j):
        at = pl.ds(r * rows, rows)
        return across(
            part.at[at], inbox.at[j - 1, at], box_send.at[j - 1, r], box_recv.at[j - 1, r], j
        )

    barrier = pltpu.get_barrier_semaphore()
    for j in range(1, lanes):
        pl.semaphore_signal(
            barrier, inc=1, device_id={"tensor": lax.rem(lane + j, lanes)}, device_id_type=MESH
        )
    for load in loads:
        load.start()
    greet(spans, ranges, lanes - 1)
    early.start()
    loads[0].wait()
    loads[1].wait()
    early.wait()
    end = pl.ds(length - 16, 16)
    last[...] = dproj[end, :mixed_width].astype(F32)
    kept = jnp.where(c == ranges - 1, jnp.zeros_like(early_in), early_in[...])
    last[8:16, :] = tail_ref[...] + kept
    dproj[end, :mixed_width] = last[...].astype(BF)
    deep = model // spans
    for k in order:
        block = flip(f, k)
        late = dot(
            normed[:, pl.ds(pl.multiple_of(block * deep, deep), deep)], dproj[...], TN
        ).astype(BF)
        src[pl.ds(block * ranges, ranges)] = late.reshape(ranges, -1, late.shape[1])
        scatter.start_halves(k)
    small.start()
    for load in loads[2:5]:
        load.wait()
    pending = list(order)
    for r in range(blocks):
        for k in pending[: -(-len(order) // blocks)]:
            scatter.start_fulls(k)
        pending = pending[-(-len(order) // blocks) :]
        at = slice(r * rows, (r + 1) * rows)
        part[at, :] = (
            dot(zb[at, :], gate[...].reshape(model, -1), NT)
            + dot(dproj[at, :], packed[...].reshape(model, -1), NT)
        ).astype(BF)
        for j in range(1, lanes):
            box(r, j).start()
    small.turn()
    for load in loads[5:]:
        load.wait()
    gain = gain_ref[...]
    own_at = pl.ds(pl.multiple_of(lane * share, share), share)
    gain_own = gain_ref[:, own_at]
    norm_sum = jnp.zeros((1, share), F32)
    sent = 0
    for r in range(blocks):
        for j in range(1, lanes):
            box(r, j).wait_recv()
        at = slice(r * rows, (r + 1) * rows)
        wide = hidden[at, :].astype(F32)
        scale = lax.rsqrt(jnp.mean(wide * wide, axis=1, keepdims=True) + EPSILON)
        whole_grad = part[at, :].astype(F32)
        own_grad = part[at, own_at].astype(F32)
        for j in range(1, lanes):
            whole_grad = whole_grad + inbox[j - 1, at, :].astype(F32)
            own_grad = own_grad + inbox[j - 1, at, own_at].astype(F32)
        inner = jnp.mean(whole_grad * gain * wide, axis=1, keepdims=True)
        own = hidden[at, own_at].astype(F32)
        grad_ref[at, :] = (
            dmix[at, own_at].astype(F32) + scale * (own_grad * gain_own)
            - own * (scale * scale * scale * inner)
        )
        norm_sum = norm_sum + jnp.sum(own_grad * own * scale, axis=0, keepdims=True)
        if r % 2 == 0 and sent < 2:
            scatter.start_far(order[sent], packed_grad)
            sent += 1
    norm_own[...] = jnp.broadcast_to(norm_sum, norm_own.shape)
    norm.start()
    for k in order[sent:]:
        if k == order[-1]:
            norm.turn()
        scatter.start_far(k, packed_grad)
    small_out[...] = small.result()
    norm_out[...] = norm.result()
    scatter.finish(packed_grad)
    high = packed_grad.shape[0]
    shared[0:high, :] = packed_grad[:, width:mixed_width]
    shared[high:, :] = small_out[0:8, width:]
    shared_in[lane] = shared[...]
    for j in range(1, lanes):
        across(shared, shared_in.at[lane], shared_send.at[j - 1], shared_recv.at[j - 1], j).start()
    for j in range(1, lanes):
        source = lax.rem(lane + lanes - j, lanes)
        across(
            shared, shared_in.at[source], shared_send.at[j - 1], shared_recv.at[j - 1], j
        ).wait_recv()
    both = shared_in[0]
    for j in range(1, lanes):
        both = both + shared_in[j]
    packed_grad[:, width:mixed_width] = both[0:high, :]
    small_out[0:8, width:] = both[high:, :]
    scatter.drain()
    small.drain()
    norm.drain()
    for j in range(1, lanes):
        across(
            shared, shared_in.at[lane], shared_send.at[j - 1], shared_recv.at[j - 1], j
        ).wait_send()
        for r in range(blocks):
            box(r, j).wait_send()


def finish(gain, tail, early, small, dproj, normed, zb, gate, packed, hidden, dmix, width, share):
    spans, ranges = lax.axis_size("fsdp"), lax.axis_size("context")
    lanes = lax.axis_size("tensor")
    length, model = hidden.shape
    mixed_width = tail.shape[1]
    rows, wide = packed.shape[1:]
    blocks = 4
    vmem = pl.BlockSpec(memory_space=pltpu.VMEM)
    anywhere = pl.BlockSpec(memory_space=pl.ANY)
    held = [dproj, normed, zb, gate, packed, hidden, dmix]
    near_sem = pltpu.SemaphoreType.DMA((ranges,))
    far_sem = pltpu.SemaphoreType.DMA((spans,))
    box_sem = pltpu.SemaphoreType.DMA((lanes - 1, blocks))
    lane_sem = pltpu.SemaphoreType.DMA((lanes - 1,))
    shared = (rows + 8, mixed_width - width)
    return pl.pallas_call(
        functools.partial(finish_kernel, spans, ranges, lanes, width, mixed_width, blocks),
        in_specs=[vmem] * 4 + [anywhere] * 7,
        out_specs=[vmem] * 4,
        out_shape=[
            jax.ShapeDtypeStruct((length, share), F32),
            jax.ShapeDtypeStruct((rows, wide), F32),
            jax.ShapeDtypeStruct(small.shape, F32),
            jax.ShapeDtypeStruct((8, share), F32),
        ],
        scratch_shapes=[pltpu.VMEM(v.shape, v.dtype) for v in held] + [
            pltpu.VMEM((spans * ranges, rows, wide), BF),
            pltpu.VMEM((length, model), BF),
            pltpu.VMEM((lanes - 1, length, model), BF),
            pltpu.VMEM((8, mixed_width), F32),
            pltpu.VMEM((16, mixed_width), F32),
            pltpu.VMEM((8, share), F32),
            pltpu.VMEM((ranges,) + small.shape, F32),
            pltpu.VMEM(small.shape, F32),
            pltpu.VMEM((spans,) + small.shape, F32),
            pltpu.VMEM((ranges, 8, share), F32),
            pltpu.VMEM((8, share), F32),
            pltpu.VMEM((spans, 8, share), F32),
            pltpu.VMEM(shared, F32),
            pltpu.VMEM((lanes,) + shared, F32),
        ] + scatter_scratch(spans, 1, rows, wide) + [
            pltpu.SemaphoreType.DMA((7,)), pltpu.SemaphoreType.DMA((2,)),
            box_sem, box_sem, lane_sem, lane_sem,
        ] + [near_sem, near_sem, far_sem, far_sem] * 2,
        compiler_params=pltpu.CompilerParams(collective_id=2, has_side_effects=True),
        name="finish",
    )(gain, tail, early, small, *held)


def ring(axis, step):
    count = lax.axis_size(axis)
    return [(source, (source + step) % count) for source in range(count)]


def shifted(value, axis, steps):
    count = lax.axis_size(axis)
    initial, last = (max(0, -steps), min(count, count - steps))
    return lax.ppermute(value, axis, [(source, source + steps) for source in range(initial, last)])


def total_over(value, axis):
    if lax.axis_size(axis) == 2:
        return value.astype(F32) + lax.ppermute(value, axis, ring(axis, 1)).astype(F32)
    return jnp.sum(gather_axis(value, axis, 0).astype(F32), axis=0)


def share_over(value, axis, dim):
    count, index = (lax.axis_size(axis), lax.axis_index(axis))
    size = value.shape[dim] // count
    part = lambda at: lax.dynamic_slice_in_dim(value, at * size, size, dim)
    result = part(index).astype(F32)
    for step in range(1, count):
        sent = part((index + step) % count)
        result = result + lax.ppermute(sent, axis, ring(axis, step)).astype(F32)
    return result


def gather_axis(value, axis, dim):
    count, index = (lax.axis_size(axis), lax.axis_index(axis))
    shape = value.shape[:dim] + (count,) + value.shape[dim:]
    result = lax.dynamic_update_index_in_dim(jnp.zeros(shape, value.dtype), value, index, dim)
    for step in range(1, count):
        got = lax.ppermute(value, axis, ring(axis, step))
        result = lax.dynamic_update_index_in_dim(result, got, (index - step) % count, dim)
    return result


def chain(state, decay_rows, direction):
    states = state.shape[0]
    packed = jnp.concatenate([state, decay_rows], axis=0).astype(BF)
    total = jnp.zeros_like(state)
    factor = jnp.ones((1, state.shape[1]), F32)
    for step in range(1, lax.axis_size("context")):
        got = shifted(packed, "context", direction * step).astype(F32)
        total = total + factor * got[:states]
        factor = factor * got[states : states + 1]
    return total


def body(
    hidden, d_mixed, seq_lengths, norm_gain, w_gate, w_x, w_bc, w_dt, conv_x, conv_x_bias,
    conv_bc, conv_bc_bias, dt_bias, a_log, d_skip, gate_gain, w_out,
):
    row_count, model_width = hidden.shape
    lanes = lax.axis_size("tensor")
    lane = lax.axis_index("tensor")
    share_width = model_width // lanes
    share_start = lane * share_width
    inner_local = conv_x.shape[1]
    inner_width = inner_local * lanes
    heads = dt_bias.shape[0]
    bc_width = conv_bc.shape[1]
    states = bc_width // 2
    lengths = seq_lengths[0]
    count = lengths.shape[0]
    first_row = lax.axis_index("context") * row_count
    starts = (jnp.cumsum(lengths) - lengths).astype(jnp.int32)
    info = jnp.concatenate([first_row.astype(jnp.int32)[None], starts[1:]])
    spread = (
        lax.broadcasted_iota(jnp.int32, (heads, inner_local), 1) // (inner_local // heads)
        == lax.broadcasted_iota(jnp.int32, (heads, inner_local), 0)
    ).astype(BF)

    widened = hidden.astype(F32)
    row_scale = lax.rsqrt(jnp.mean(widened * widened, axis=1, keepdims=True) + EPSILON)
    mixed_width = inner_local + bc_width
    spare = -(-heads // 128) * 128 - heads
    packed = jnp.concatenate(
        [w_x, w_bc, w_dt, jnp.zeros((w_x.shape[0], spare), w_x.dtype)], axis=1
    )
    bias_row, alog_row, skip_row = (dt_bias[None, :], a_log[None, :], d_skip[None, :])
    taps_all = jnp.concatenate([conv_x, conv_bc], axis=1)
    (
        normed, proj, edge, x_act, bc_act, slope, y_local, full, states_at, final,
        packed_all, gate_all, out_all,
    ) = forward(
        info, count, hidden, norm_gain[None, :], packed, w_gate, w_out.T,
        taps_all,
        jnp.concatenate([conv_x_bias, conv_bc_bias])[None, :],
        bias_row, alog_row, spread,
    )
    gate_weight = gate_all.reshape(model_width, -1)
    out_weight = out_all.reshape(model_width, -1)
    z_proj = dot(normed, gate_weight).astype(BF)
    decay_rows = final[states:]
    state_in = chain(final[:states], decay_rows, 1)
    c_rows = bc_act[:, states:]
    full_wide = expand(full, spread)
    y = y_local + dot(c_rows, state_in.astype(BF)) * full_wide
    skip_wide = jnp.repeat(d_skip, inner_local // heads)[None, :]
    y_full = y + skip_wide * x_act.astype(F32)
    z = z_proj.astype(F32)
    sig = jax.nn.sigmoid(z)
    gate = z * sig
    gated = y_full * gate
    grad_norm_out = dot(d_mixed, out_weight)
    scaled = grad_norm_out * gate_gain[None, :]
    both = total_over(
        jnp.stack([jnp.sum(gated * gated, axis=1), jnp.sum(scaled * gated, axis=1)]), "tensor"
    )
    gate_scale = lax.rsqrt(both[0][:, None] / inner_width + EPSILON)
    unit = gated * gate_scale
    normed_out = (unit * gate_gain[None, :]).astype(BF)
    grad_gated = gate_scale * scaled - gated * gate_scale**3 * (both[1][:, None] / inner_width)
    dy = (grad_gated * gate).astype(BF)
    grad_zb = (grad_gated * y_full * sig * (1.0 + z * (1.0 - sig))).astype(BF)
    gain_term = jnp.sum(grad_norm_out * unit, axis=0)
    grad_in = dot(c_rows, (dy.astype(F32) * full_wide).astype(BF), TN)
    leaving = chain(grad_in, decay_rows, -1)
    out_partial = dot(normed_out, out_weight, NT).astype(BF)
    out_term = dot(d_mixed, normed_out, TN).astype(BF)
    gate_term = dot(normed, grad_zb, TN).astype(BF)
    leaving, out_partial, out_term, gate_term = lax.optimization_barrier(
        (leaving, out_partial, out_term, gate_term)
    )
    mixed_share = share_over(out_partial, "tensor", 1)
    hidden_share = lax.dynamic_slice_in_dim(widened, share_start, share_width, 1)
    mixed = (hidden_share + mixed_share).astype(BF)
    by_owner = lambda v: v.reshape(-1, w_gate.shape[0], v.shape[1])
    starting = jnp.concatenate([jnp.ones((1, heads), F32), full[CHUNK - 1 :: CHUNK][:-1]], axis=0)
    starting = jnp.broadcast_to(starting[:, None, :], (starting.shape[0], 8, heads))
    dproj, tail, early, conv_grads, head_sums, grad_w_out, grad_w_gate = backward(
        info, count, x_act, bc_act, slope, proj, edge, taps_all, bias_row, alog_row, skip_row,
        spread, y, dy, states_at, starting, state_in, leaving,
        by_owner(out_term), by_owner(gate_term),
    )
    grad_w_out = grad_w_out.T
    small = jnp.concatenate(
        [
            conv_grads,
            jnp.pad(head_sums[:3], ((0, 0), (0, mixed_width - heads))),
            jnp.pad(gain_term[None, :], ((0, 4), (0, bc_width))),
        ],
        axis=0,
    )
    grad_hidden, grad_packed, small, snorm = finish(
        norm_gain[None, :], tail, early, small, dproj, normed, grad_zb, gate_all, packed_all,
        hidden, d_mixed, inner_local, share_width,
    )
    taps = conv_x.shape[0]
    sx, sbc = small[: taps + 1, :inner_local], small[: taps + 1, inner_local:]
    sh = small[8:11, :heads]
    sgain = small[11, :inner_local]
    snorm = snorm[0]
    grad_bc = grad_packed[:, inner_local:mixed_width]
    grad_w_x = grad_packed[:, :inner_local]
    grad_w_dt = grad_packed[:, mixed_width : mixed_width + heads]
    return (
        mixed, grad_hidden, snorm, grad_w_gate, grad_w_x, grad_bc, grad_w_dt, sx[:taps], sx[taps], sbc[:taps], sbc[taps],
        sh[0], sh[1], sh[2], sgain, grad_w_out,
    )


def solution(mesh):
    return jax.shard_map(
        body,
        mesh=mesh,
        in_specs=(
            P(("fsdp", "context"), None),
            P(("fsdp", "context"), None),
            P("fsdp", None),
            P(),
            P(("fsdp", "context"), "tensor"),
            P(("fsdp", "context"), "tensor"),
            P(("fsdp", "context"), None),
            P(("fsdp", "context"), "tensor"),
            P(None, "tensor"),
            P("tensor"),
            P(),
            P(),
            P("tensor"),
            P("tensor"),
            P("tensor"),
            P("tensor"),
            P("tensor", ("fsdp", "context")),
        ),
        out_specs=(
            P(("fsdp", "context"), "tensor"),
            P(("fsdp", "context"), "tensor"),
            P("tensor"),
            P(("fsdp", "context"), "tensor"),
            P(("fsdp", "context"), "tensor"),
            P(("fsdp", "context"), None),
            P(("fsdp", "context"), "tensor"),
            P(None, "tensor"),
            P("tensor"),
            P(),
            P(),
            P("tensor"),
            P("tensor"),
            P("tensor"),
            P("tensor"),
            P("tensor", ("fsdp", "context")),
        ),
        check_vma=False,
    )
```
